128 devices in a mesh: gx: 4 (over z), gy: 4 (over x), gz: 8 (over y, core).
Axes of the slice: x: 4, y: 4, z: 4, core: 2. Of those that a mesh axis runs over, the one named last changes fastest.
Arguments:
- pressure: float32 [128, 128, 1024], P('gx', 'gy', 'gz'), may hold values from -6 to 6
- saturation: float32 [2, 128, 128, 1024], P(None, 'gx', 'gy', 'gz'), may hold values from 0.05 to 0.45
- old_saturation: float32 [2, 128, 128, 1024], P(None, 'gx', 'gy', 'gz'), may hold values from 0.05 to 0.45
- permeability: float32 [128, 128, 1024], P('gx', 'gy', 'gz'), may hold values from 0.1 to 10
- storage: float32 [128, 128, 1024], P('gx', 'gy', 'gz'), may hold values from 0.3 to 3
- cell_mask: int32 [128, 128, 1024], P('gx', 'gy', 'gz'), may hold values from 0 to 1, as said below
- row_owner: int32 [128, 128, 8], P('gx', 'gy', 'gz'), may hold values from -1 to 127, as said below
- row_slot: int32 [128, 128, 8], P('gx', 'gy', 'gz'), may hold values from -1 to 639, as said below
Outputs:
- update: float32 [3, 81920, 128], P(None, ('gx', 'gy', 'gz'))
The draws below stay inside these ranges and needn't reach their ends.
Inputs may be any that keep to these rules, and one draw needn't show every extreme that they name: `cell_mask`: A block row of 128 cells without an active cell has row_owner -1; every other block row has an owner. `row_owner`: -1 exactly for block rows without active cells; every owner holds exactly 640 block rows; at most 8 block rows of one device's tile go to one owner, and in every draw some tile sends exactly 8 to every owner. `row_slot`: -1 exactly where row_owner is -1; the places of one owner's block rows are 0 to 639, each taken once.
All inputs are finite; a program needn't handle non-finite values.
Results may differ from the reference program's by a relative error of at most 0.0003.
Values sent between devices are 32-bit elements; how exact they have to be, the bound alone decides.
No kernel may reach another device: no remote copies, remote signals or barrier semaphores. Data moves between devices by JAX's collectives and lax.ppermute only.
A program may use at most 128 MiB of HBM per device.

```python
import math
import jax
import jax.numpy as jnp

CX = 32
CY = 32
LINE = 128
ITERS = 2
SWEEPS = 4
NX = 128
NY = 128
ZBLK = 8
NZ = 1024
NDEV = 128
SLOTS = 640


def block_layout(key):
    base_key = jax.random.fold_in(key, 7301)
    key_level, key_full, key_score, key_anchor, key_keep = jax.random.split(base_key, 5)
    rows_dev = CX * CY
    levels = jax.random.randint(key_level, (NDEV,), 0, 4)
    chosen = jax.random.randint(key_full, (), 0, NDEV)
    levels = jnp.where(jnp.arange(NDEV, dtype=jnp.int32) == chosen, 6, levels)
    scores = levels[:, None] * 1048576 + jax.random.randint(key_score, (NDEV, rows_dev), 0, 1048576)
    ranking = jnp.argsort(-scores.reshape(NDEV * rows_dev), stable=True)
    live_rows = jnp.zeros((NDEV * rows_dev,), jnp.int32).at[ranking[:NDEV * SLOTS]].set(1)
    live_rank = jnp.cumsum(live_rows) - 1
    owners = jnp.where(live_rows > 0, live_rank % NDEV, -1).astype(jnp.int32)
    places = jnp.where(live_rows > 0, live_rank // NDEV, -1).astype(jnp.int32)
    keep_cell = (jax.random.randint(key_keep, (NDEV * rows_dev, LINE), 0, 16) > 0).astype(jnp.int32)
    anchor = jax.random.randint(key_anchor, (NDEV * rows_dev, 1), 0, LINE)
    keep_cell = jnp.maximum(keep_cell, (jnp.arange(LINE, dtype=jnp.int32)[None, :] == anchor).astype(jnp.int32))
    cell_grid = keep_cell * live_rows[:, None]
    grid_x = NX // CX
    grid_y = NY // CY
    cell_grid = cell_grid.reshape(grid_x, grid_y, ZBLK, CX, CY, LINE).transpose(0, 3, 1, 4, 2, 5).reshape(NX, NY, NZ)
    owners = owners.reshape(grid_x, grid_y, ZBLK, CX, CY).transpose(0, 3, 1, 4, 2).reshape(NX, NY, ZBLK)
    places = places.reshape(grid_x, grid_y, ZBLK, CX, CY).transpose(0, 3, 1, 4, 2).reshape(NX, NY, ZBLK)
    return (cell_grid.astype(jnp.int32), owners, places)


def draw_cell_mask(key, part):
    return block_layout(key)[0]


def draw_row_owner(key, part):
    return block_layout(key)[1]


def draw_row_slot(key, part):
    return block_layout(key)[2]


def shard_levels(stream_key, shape, pieces, low, top_value):
    loudness = 1.0
    for dim, parts in pieces:
        heights = jax.random.uniform(jax.random.fold_in(jax.random.fold_in(stream_key, 6), dim), (parts,), jnp.float32, low / len(pieces), top_value / len(pieces))
        loudness = loudness * jnp.repeat(jnp.exp(heights), shape[dim] // parts).reshape((-1,) + (1,) * (len(shape) - 1 - dim))
    return loudness


def noise(rng, extent, scale, most, cuts=(), kind=jnp.bfloat16):
    result = jax.random.normal(rng, extent, jnp.float32) * scale
    if len(cuts) > 0:
        result = shard_levels(rng, extent, cuts, -0.22, 0.18) * result
    return jnp.clip(result, min=-most, max=most).astype(kind)


def setup_inputs(seed: int = 0) -> dict:
    keys = jax.random.split(jax.random.key(seed), 9)
    return {
        "pressure": noise(keys[0], (NX, NY, NZ), 1.0, 6.0, ((0, 4), (1, 4), (2, 8)), jnp.float32),
        "saturation": jnp.clip(0.05 + 0.39999999 * jax.random.uniform(keys[1], (2, NX, NY, NZ), jnp.float32) ** shard_levels(keys[1], (2, NX, NY, NZ), ((1, 4), (2, 4), (3, 8)), -0.2, 0.2), 0.05, 0.45),
        "old_saturation": jnp.clip(0.05 + 0.39999999 * jax.random.uniform(keys[2], (2, NX, NY, NZ), jnp.float32) ** shard_levels(keys[2], (2, NX, NY, NZ), ((1, 4), (2, 4), (3, 8)), -0.2, 0.2), 0.05, 0.45),
        "permeability": jnp.clip(jnp.exp(math.log(10.0) - 4.6051702 * jax.random.uniform(keys[3], (NX, NY, NZ), jnp.float32) ** shard_levels(keys[3], (NX, NY, NZ), ((0, 4), (1, 4), (2, 8)), -0.2, 0.2)), 0.1, 10.0),
        "storage": jnp.clip(jnp.exp(math.log(3.0) - 2.3025851 * jax.random.uniform(keys[4], (NX, NY, NZ), jnp.float32) ** shard_levels(keys[4], (NX, NY, NZ), ((0, 4), (1, 4), (2, 8)), -0.2, 0.2)), 0.3, 3.0),
        "cell_mask": draw_cell_mask(jax.random.fold_in(keys[8], 71), 0),
        "row_owner": draw_row_owner(jax.random.fold_in(keys[8], 71), 0),
        "row_slot": draw_row_slot(jax.random.fold_in(keys[8], 71), 0),
    }


VISCOSITY = (0.5, 2.0, 0.25)
COMPRESS = (0.5, 1.0, 2.0)


def shifted(padded):
    return [padded[..., 2:, 1:-1, 1:-1], padded[..., :-2, 1:-1, 1:-1],
            padded[..., 1:-1, 2:, 1:-1], padded[..., 1:-1, :-2, 1:-1],
            padded[..., 1:-1, 1:-1, 2:], padded[..., 1:-1, 1:-1, :-2]]


def phases_of(saturation):
    return jnp.stack([saturation[0], 1.0 - saturation[0] - saturation[1], saturation[1]])


def mobilities(saturation):
    phase_sat = phases_of(saturation)
    viscous = jnp.array(VISCOSITY, jnp.float32).reshape(3, 1, 1, 1)
    return phase_sat * phase_sat / viscous


def assemble(pressure, saturation, old_saturation, conduct, storage, active, mobility, padded):
    flux_sum = jnp.zeros_like(mobility)
    couple_list = []
    for neighbour in shifted(padded):
        transmit = 2.0 * conduct * neighbour[1] / jnp.maximum(conduct + neighbour[1], 0.5)
        upwind = jnp.where(pressure >= neighbour[0], mobility, neighbour[2:])
        weight = transmit * upwind
        couple_list.append(weight)
        flux_sum = flux_sum + weight * (pressure - neighbour[0])
    outflow = couple_list[0]
    for face_index in range(1, 6):
        outflow = outflow + couple_list[face_index]
    change = saturation - old_saturation
    phase_change = jnp.stack([change[0], -change[0] - change[1], change[1]])
    compress = jnp.array(COMPRESS, jnp.float32).reshape(3, 1, 1, 1)
    press_column = active * (storage * compress * phases_of(saturation) + outflow) + (1.0 - active)
    sat_scale = active * storage + (1.0 - active)
    right_side = -(active * storage * phase_change + flux_sum)
    return right_side, press_column, sat_scale, couple_list


def precondition(right_side, press_column, sat_scale, phase_terms, press_terms):
    press_total = jnp.sum(press_column, axis=0)
    sol_press = jnp.zeros_like(sat_scale)
    sol_water = jnp.zeros_like(sat_scale)
    sol_gas = jnp.zeros_like(sat_scale)
    for outer_index in range(ITERS):
        if outer_index == 0:
            residual = right_side
        else:
            applied = press_column * sol_press + sat_scale * jnp.stack([sol_water, -sol_water - sol_gas, sol_gas]) - phase_terms(sol_press)
            residual = right_side - applied
        reduced = jnp.sum(residual, axis=0)
        correction = reduced / press_total
        for sweep_index in range(SWEEPS - 1):
            correction = correction + ((reduced - press_total * correction) + press_terms(correction)) / press_total
        second = residual - (press_column * correction - phase_terms(correction))
        lifted = jnp.sum(second, axis=0) / press_total
        sol_press = sol_press + correction + lifted
        sol_water = sol_water + (second[0] - press_column[0] * lifted) / sat_scale
        sol_gas = sol_gas + (second[2] - press_column[2] * lifted) / sat_scale
    return jnp.stack([sol_press, sol_water, sol_gas])


def reference(pressure, saturation, old_saturation, permeability, storage, cell_mask, row_owner, row_slot):
    active = cell_mask.astype(jnp.float32)
    conduct = permeability * active
    mobility = mobilities(saturation)
    fields = jnp.concatenate([pressure[None], conduct[None], mobility], axis=0)
    padded = jnp.pad(fields, ((0, 0), (1, 1), (1, 1), (1, 1)))
    right_side, press_column, sat_scale, couple_list = assemble(pressure, saturation, old_saturation, conduct, storage, active, mobility, padded)
    press_list = [jnp.sum(weight, axis=0) for weight in couple_list]

    def phase_terms(values):
        nearby = shifted(jnp.pad(values, 1))
        summed = couple_list[0] * nearby[0]
        for face_index in range(1, 6):
            summed = summed + couple_list[face_index] * nearby[face_index]
        return summed

    def press_terms(values):
        nearby = shifted(jnp.pad(values, 1))
        summed = press_list[0] * nearby[0]
        for face_index in range(1, 6):
            summed = summed + press_list[face_index] * nearby[face_index]
        return summed

    solution = precondition(right_side, press_column, sat_scale, phase_terms, press_terms)
    block_rows = solution.reshape(3, NX * NY * ZBLK, LINE)
    owner_rows = row_owner.reshape(NX * NY * ZBLK)
    slot_rows = row_slot.reshape(NX * NY * ZBLK)
    position = jnp.where(owner_rows >= 0, owner_rows * SLOTS + slot_rows, NDEV * SLOTS).astype(jnp.int32)
    return jnp.zeros((3, NDEV * SLOTS, LINE), jnp.float32).at[:, position].set(block_rows, mode="drop")
```

```python
import jax
import jax.numpy as jnp
from jax import lax
from jax.experimental import pallas as pl
from jax.experimental.pallas import tpu as pltpu
from jax.sharding import PartitionSpec as P

AXES = ("gx", "gy", "gz")
F32 = jnp.float32
T = 32
L = 128
H = 10
OJ = 12
EI = T + 2 * H
EJ = 56
SWEEPS = 9
SLOTS = 640
ZG = 10
ZS = 12
VMEM_LIMIT = 60 * 1024 * 1024


def strip_offsets():
    offsets, at = {}, 0
    for side in (0, 1):
        for dist in range(1, H):
            offsets[side, dist] = at
            at += H - dist
    return offsets


STRIPS = strip_offsets()


def plane_of(side, dist):
    return H - dist if side == 0 else dist - 1


def prep_kernel(p, sat, perm, sto, mask, own, xm, xp, ym, yp):
    def rows(q, carry):
        for u in range(4):
            i = q * 4 + u
            act = mask[i].astype(F32)
            s_w, s_g = sat[0, i], sat[1, i]
            s_o = 1.0 - s_w - s_g
            m_w, m_o, m_g = s_w * s_w * 2.0, s_o * s_o * 0.5, s_g * s_g * 4.0
            lam = m_w + m_o + m_g
            cond = perm[i] * act
            diag = act * (sto[i] * (0.5 * s_w + s_o + 2.0 * s_g)) + 3.0 * (1.0 - act)
            a_w, a_g = m_w / lam, m_g / lam
            for f, v in enumerate((cond, lam, diag, a_w, a_g)):
                own[f, i] = v
            for f, v in enumerate((p[i], cond, lam, diag)):
                ym[f * 8 + q, 10 * u : 10 * u + 10] = v[:H]
                yp[f * 8 + q, 10 * u : 10 * u + 10] = v[T - H :]
            for f, v in enumerate((a_w, a_g)):
                ym[32 + f, pl.ds(i, 1)] = v[:1]
                yp[32 + f, pl.ds(i, 1)] = v[T - 1 :]
        return carry

    lax.fori_loop(0, 8, rows, 0)
    for f in range(4):
        for t in range(H):
            xm[f * H + t] = p[t] if f == 0 else own[f - 1, t]
            xp[f * H + t] = p[T - H + t] if f == 0 else own[f - 1, T - H + t]
    for f in range(2):
        xm[4 * H + f] = own[3 + f, 0]
        xp[4 * H + f] = own[3 + f, T - 1]


def strip_kernel(x_lo, x_hi, cm, cp):
    for f in range(4):
        for side, src in ((0, x_lo), (1, x_hi)):
            for dist in range(1, H):
                n, at = H - dist, STRIPS[side, dist]
                t = f * H + plane_of(side, dist)
                cm[f, at : at + n] = src[t, :n]
                cp[f, at : at + n] = src[t, T - n :]


def lanes_of(rows):
    return lax.broadcasted_iota(jnp.int32, (rows, L), 1)


def build_kernel(edge, p, own, x_lo, x_hi, y_lo, y_hi, c_lo, c_hi, ext, aext, zm, zp):
    def cells(q, carry):
        for u in range(4):
            i = q * 4 + u
            for f in range(4):
                lo = y_lo[f * 8 + q, 10 * u : 10 * u + 10]
                hi = y_hi[f * 8 + q, 10 * u : 10 * u + 10]
                if f == 1:
                    lo, hi = lo * edge[2], hi * edge[3]
                ext[f, H + i, OJ - H : OJ] = lo
                ext[f, H + i, OJ : OJ + T] = p[i] if f == 0 else own[f - 1, i]
                ext[f, H + i, OJ + T : OJ + T + H] = hi
            for f in range(2):
                aext[f, 1 + i, OJ - 1 : OJ] = y_lo[32 + f, pl.ds(i, 1)]
                aext[f, 1 + i, OJ : OJ + T] = own[3 + f, i]
                aext[f, 1 + i, OJ + T : OJ + T + 1] = y_hi[32 + f, pl.ds(i, 1)]
        return carry

    lax.fori_loop(0, 8, cells, 0)
    for f in range(4):
        for side, src in ((0, x_lo), (1, x_hi)):
            for dist in range(1, H + 1):
                t = plane_of(side, dist)
                i = t if side == 0 else H + T + t
                v = src[f * H + t]
                if f == 1:
                    v = v * edge[side]
                ext[f, i, OJ : OJ + T] = v
                n = H - dist
                if n:
                    at = STRIPS[side, dist]
                    lo, hi = c_lo[f, at : at + n], c_hi[f, at : at + n]
                    if f == 1:
                        lo, hi = lo * (edge[side] * edge[2]), hi * (edge[side] * edge[3])
                    ext[f, i, OJ - n : OJ] = lo
                    ext[f, i, OJ + T : OJ + T + n] = hi
    for f in range(2):
        aext[f, 0, OJ : OJ + T] = x_lo[4 * H + f]
        aext[f, T + 1, OJ : OJ + T] = x_hi[4 * H + f]
    lane = lanes_of(EJ)

    def pack(s, carry):
        f, q = s // 5, s % 5
        low = jnp.zeros((EJ, L), F32)
        high = low
        for g in range(ZG):
            r = ext[f, 1 + q * ZG + g]
            if g:
                r = pltpu.roll(r, ZS * g, 1)
            low = jnp.where((lane >= ZS * g) & (lane < ZS * g + H), r, low)
            first = (ZS * g - H) % L
            high = jnp.where((lane >= first) & (lane < first + H), r, high)
        zm[s] = low
        zp[s] = high
        return carry

    lax.fori_loop(0, 20, pack, 0)

    def pack_share(f, carry):
        low = jnp.zeros((EJ, L), F32)
        high = low
        for g in range(T):
            r = aext[f, 1 + g]
            if g:
                r = pltpu.roll(r, g, 1)
            low = jnp.where(lane == g, r, low)
            high = jnp.where(lane == (g + L - 1) % L, r, high)
        zm[20 + f] = low
        zp[20 + f] = high
        return carry

    lax.fori_loop(0, 2, pack_share, 0)


def face(p, c, m, pn, cn, mn):
    trans = 2.0 * c * cn / jnp.maximum(c + cn, 0.5)
    there = trans * jnp.where(p >= pn, m, mn)
    back = trans * jnp.where(pn >= p, mn, m)
    step = pn - p
    return there, back, there * step, back * step


def solve_kernel(
    edge, dst, ext, aext, z_lo, z_hi, sat, old, sto, mask, places, send,
    wide, mat, base, one, two, total, rows, stage, sem,
):
    lane = lanes_of(EJ)
    at_end, at_start = lane == L - 1, lane == 0

    def spread(s, carry):
        f, q = s // 5, s % 5
        right, left = z_hi[s], z_lo[s]
        scale = jnp.where(lane < L // 2, edge[5], edge[4])
        scale = jnp.where(f == 1, scale, 1.0)
        for g in range(ZG):
            r, l = right, left
            if g:
                r, l = pltpu.roll(r, L - ZS * g, 1), pltpu.roll(l, L - ZS * g, 1)
            wide[f, 1 + q * ZG + g] = jnp.where(lane < L // 2, r, l) * scale
        return carry

    lax.fori_loop(0, 20, spread, 0)

    def pair(ref, *index):
        return ref[(0,) + index], ref[(1,) + index]

    def ring_next(a, w, end):
        ra, rw = pltpu.roll(a, L - 1, 1), pltpu.roll(w, L - 1, 1)
        return jnp.where(end, rw, ra), jnp.where(end, ra, rw)

    def ring_prev(a, w, start):
        ra, rw = pltpu.roll(a, 1, 1), pltpu.roll(w, 1, 1)
        return jnp.where(start, rw, ra), jnp.where(start, ra, rw)

    def up(v):
        return pltpu.roll(v, v.shape[0] - 1, 0)

    def down(v):
        return pltpu.roll(v, 1, 0)

    def both(f, i):
        return ext[f, i], wide[f, i]

    def x_face(i):
        here = [both(f, i) for f in range(3)]
        nxt = [both(f, i + 1) for f in range(3)]
        return [
            face(*(h[t] for h in here), *(n[t] for n in nxt)) for t in (0, 1)
        ]

    def assemble(i, carry):
        fields = [both(f, i) for f in range(3)]
        cross = x_face(i)
        nz = [ring_next(*v, at_end) for v in fields]
        z_faces = [face(*(v[t] for v in fields), *(n[t] for n in nz)) for t in (0, 1)]
        z_back = ring_prev(z_faces[0][1], z_faces[1][1], at_start)
        z_flow = ring_prev(z_faces[0][3], z_faces[1][3], at_start)
        out = []
        for t in (0, 1):
            mine = [v[t] for v in fields]
            y_there, y_back, y_flow, y_bflow = face(*mine, *(up(v) for v in mine))
            y_back, y_bflow = down(y_back), down(y_bflow)
            x_there, x_back, x_flow, x_bflow = cross[t]
            z_there, _, z_out, _ = z_faces[t]
            whole = both(3, i)[t] + (x_there + carry[2 * t]) + (y_there + y_back) + (z_there + z_back[t])
            flow = (x_flow - carry[2 * t + 1]) + (y_flow - y_bflow) + (z_out - z_flow[t])
            inv = 1.0 / whole
            weights = (x_there, carry[2 * t], y_there, y_back, z_there, z_back[t])
            for k, w in enumerate(weights):
                mat[k, t, i] = w * inv
            base[t, i] = flow * inv
            if t == 0:
                total[i] = whole
            out += [x_back, x_bflow]
        return tuple(out)

    first = x_face(0)
    lax.fori_loop(
        1, EI - 1, assemble, (first[0][1], first[0][3], first[1][1], first[1][3])
    )

    def sweep(src, target, depth):
        rows_at = slice(0, EJ) if depth > 3 else slice(8, 48)
        count = rows_at.stop - rows_at.start
        end, start = at_end[:count], at_start[:count]

        def plane(i, carry):
            ya, yw = src[0, i, rows_at], src[1, i, rows_at]
            zn = ring_next(ya, yw, end)
            zb = ring_prev(ya, yw, start)
            for t, y in ((0, ya), (1, yw)):
                if t == 1 and depth == 0:
                    continue
                acc = base[t, i, rows_at] + mat[0, t, i, rows_at] * src[t, i + 1, rows_at]
                acc = acc + mat[1, t, i, rows_at] * src[t, i - 1, rows_at]
                acc = acc + mat[2, t, i, rows_at] * up(y)
                acc = acc + mat[3, t, i, rows_at] * down(y)
                acc = acc + mat[4, t, i, rows_at] * zn[t]
                target[t, i, rows_at] = acc + mat[5, t, i, rows_at] * zb[t]
            return carry

        lax.fori_loop(H - depth, H + T + depth, plane, 0)

    src = base
    for k in range(1, SWEEPS + 1):
        target = one if k % 2 else two
        sweep(src, target, SWEEPS - k)
        src = target

    mid = slice(8, 48)
    end, start = at_end[:40], at_start[:40]

    def finish(i, carry):
        e = i + H
        pa, pw = ext[0, e, mid], wide[0, e, mid]
        sa, sw8 = two[0, e, mid], two[1, e, mid]
        p_near = (
            ext[0, e + 1, mid], ext[0, e - 1, mid], up(pa), down(pa),
            ring_next(pa, pw, end)[0], ring_prev(pa, pw, start)[0],
        )
        s_near = (
            two[0, e + 1, mid], two[0, e - 1, mid], up(sa), down(sa),
            ring_next(sa, sw8, end)[0], ring_prev(sa, sw8, start)[0],
        )
        share = []
        for f in range(2):
            a = aext[f, i + 1, mid]
            right = pltpu.roll(z_hi[20 + f, mid], L - 1 - i, 1)
            left = pltpu.roll(z_lo[20 + f, mid], (L + 1 - i) % L, 1)
            share.append((
                a,
                (
                    aext[f, i + 2, mid], aext[f, i, mid], up(a), down(a),
                    jnp.where(end, right, pltpu.roll(a, L - 1, 1)),
                    jnp.where(start, left, pltpu.roll(a, 1, 1)),
                ),
            ))
        sums = [jnp.zeros((40, L), F32) for _ in range(4)]
        for k in range(6):
            weight = mat[k, 0, e, mid]
            upstream = pa >= p_near[k]
            drive = s_near[k] - (pa - p_near[k])
            for f in range(2):
                w = weight * jnp.where(upstream, share[f][0], share[f][1][k])
                sums[2 * f] = sums[2 * f] + w
                sums[2 * f + 1] = sums[2 * f + 1] + w * drive
        scale = total[e, mid]
        sums = [(v * scale)[4:36] for v in sums]
        x_p = one[0, e, OJ : OJ + T]
        act = mask[i].astype(F32)
        held = act * sto[i]
        sat_scale = held + (1.0 - act)
        stage[0, i] = x_p
        for f, compress in ((0, 0.5), (1, 2.0)):
            column = held * compress * sat[f, i] + sums[2 * f] + (1.0 - act)
            change = held * (sat[f, i] - old[f, i])
            stage[1 + f, i] = (sums[2 * f + 1] - change - column * x_p) / sat_scale
        return carry

    lax.fori_loop(0, T, finish, 0)

    devices = places.shape[0]
    capacity = T * T // devices
    chunk = 3 * capacity + 1

    def place(i, carry):
        for j in range(T):
            d = dst[i * T + j]
            for f in range(3):
                rows[pl.ds(d + f * capacity, 1)] = stage[f, i, j : j + 1]
        return carry

    lax.fori_loop(0, T, place, 0)

    def tail(d, carry):
        rows[pl.ds(d * chunk + 3 * capacity, 1)] = places[pl.ds(d, 1)]
        return carry

    lax.fori_loop(0, devices, tail, 0)
    copy = pltpu.make_async_copy(rows.at[: devices * chunk], send, sem)
    copy.start()
    copy.wait()


def index_kernel(owner, slot, dst, place, count):
    devices = count.shape[0]
    capacity = T * T // devices
    chunk = 3 * capacity + 1

    def clear(d, carry):
        count[d] = 0
        return carry

    def blank(d, carry):
        place[d] = -1
        return carry

    lax.fori_loop(0, devices, clear, 0)
    lax.fori_loop(0, T * T, blank, 0, unroll=8)

    def row(r, carry):
        o = owner[r]

        @pl.when(o >= 0)
        def _():
            n = count[o]
            count[o] = n + 1
            place[o * capacity + n] = slot[r]
            dst[r] = o * chunk + n

        @pl.when(o < 0)
        def _():
            dst[r] = devices * chunk

        return carry

    lax.fori_loop(0, T * T, row, 0)


def unpack_kernel(got, update, held, number, table, where, sem):
    devices = where.shape[0]
    capacity = T * T // devices
    chunk = 3 * capacity + 1

    def collect(d, carry):
        number[pl.ds(d, 1)] = got[pl.ds(d * chunk + 3 * capacity, 1)]
        return carry

    lax.fori_loop(0, devices, collect, 0, unroll=8)
    slots = number[...].astype(jnp.int32)
    table[...] = jnp.where(slots < 0, SLOTS, slots)
    copy = pltpu.make_async_copy(table, where, sem)
    copy.start()
    copy.wait()

    def scatter(d, carry):
        for k in range(capacity):
            s = where[d, k]
            for f in range(3):
                held[f, pl.ds(s, 1)] = got[pl.ds(d * chunk + f * capacity + k, 1)]
        return carry

    lax.fori_loop(0, devices, scatter, 0)
    copy = pltpu.make_async_copy(held.at[:, :SLOTS], update, sem)
    copy.start()
    copy.wait()


def spec(space):
    return pl.BlockSpec(memory_space=space)


def shape(*dims):
    return jax.ShapeDtypeStruct(dims, F32)


def call(kernel, name, out_shape, smem, count, out_spaces=None, scratch=()):
    many = isinstance(out_shape, (tuple, list))
    spaces = out_spaces or ([pltpu.VMEM] * len(out_shape) if many else pltpu.VMEM)
    return pl.pallas_call(
        kernel,
        name=name,
        out_shape=out_shape,
        in_specs=[spec(pltpu.SMEM)] * smem + [spec(pltpu.VMEM)] * count,
        out_specs=[spec(s) for s in spaces] if many else spec(spaces),
        scratch_shapes=list(scratch),
        compiler_params=pltpu.CompilerParams(vmem_limit_bytes=VMEM_LIMIT),
    )


def ring(axis, step):
    size = lax.axis_size(axis)
    return [(i, (i + step) % size) for i in range(size)]


def swap(low, high, axis):
    return lax.ppermute(high, axis, ring(axis, 1)), lax.ppermute(low, axis, ring(axis, -1))


def body(
    pressure, saturation, old_saturation, permeability, storage, cell_mask, row_owner, row_slot
):
    devices = lax.axis_size(AXES)
    capacity = T * T // devices
    chunk = 3 * capacity + 1
    inside = []
    for axis in AXES:
        at = lax.axis_index(axis)
        inside += [at > 0, at < lax.axis_size(axis) - 1]
    edge = jnp.stack(inside).astype(F32)

    own, xm, xp, ym, yp = call(
        prep_kernel,
        "prep",
        (
            shape(5, T, T, L),
            shape(4 * H + 2, T, L),
            shape(4 * H + 2, T, L),
            shape(34, 40, L),
            shape(34, 40, L),
        ),
        0,
        5,
    )(pressure, saturation, permeability, storage, cell_mask)
    x_lo, x_hi = swap(xm, xp, "gx")
    y_lo, y_hi = swap(ym, yp, "gy")

    ints = jax.ShapeDtypeStruct((T * T,), jnp.int32)
    dst, place = call(
        index_kernel,
        "index",
        (ints, ints),
        2,
        0,
        [pltpu.SMEM] * 2,
        [pltpu.SMEM((devices,), jnp.int32)],
    )(row_owner.reshape(T * T), row_slot.reshape(T * T))
    places = jnp.pad(
        place.reshape(devices, capacity).astype(F32), ((0, 0), (0, L - capacity))
    )

    cm, cp = call(strip_kernel, "strip", (shape(4, 96, L), shape(4, 96, L)), 0, 2)(x_lo, x_hi)
    c_lo, c_hi = swap(cm, cp, "gy")
    ext, aext, zm, zp = call(
        build_kernel,
        "build",
        (shape(4, EI, EJ, L), shape(2, T + 2, EJ, L), shape(22, EJ, L), shape(22, EJ, L)),
        1,
        8,
    )(edge, pressure, own, x_lo, x_hi, y_lo, y_hi, c_lo, c_hi)
    z_lo, z_hi = swap(zm, zp, "gz")
    grid = (EI, EJ, L)
    send = call(
        solve_kernel,
        "solve",
        shape(devices * chunk, L),
        2,
        9,
        pl.ANY,
        [
            pltpu.VMEM((4,) + grid, F32),
            pltpu.VMEM((6, 2) + grid, F32),
            pltpu.VMEM((2,) + grid, F32),
            pltpu.VMEM((2,) + grid, F32),
            pltpu.VMEM((2,) + grid, F32),
            pltpu.VMEM(grid, F32),
            pltpu.VMEM((devices * chunk + 2 * capacity + 8, L), F32),
            pltpu.VMEM((3, T, T, L), F32),
            pltpu.SemaphoreType.DMA(()),
        ],
    )(edge, dst, ext, aext, z_lo, z_hi, saturation, old_saturation, storage, cell_mask, places)
    got = lax.all_to_all(
        send.reshape(devices, chunk, 1, L), AXES, split_axis=0, concat_axis=0, tiled=True
    )
    return call(
        unpack_kernel,
        "unpack",
        shape(3, SLOTS, L),
        0,
        1,
        pl.ANY,
        [
            pltpu.VMEM((3, SLOTS + 8, L), F32),
            pltpu.VMEM((devices, L), F32),
            pltpu.VMEM((devices, L), jnp.int32),
            pltpu.SMEM((devices, L), jnp.int32),
            pltpu.SemaphoreType.DMA(()),
        ],
    )(got.reshape(devices * chunk, L))


def solution(mesh):
    cells = P("gx", "gy", "gz")
    pair = P(None, "gx", "gy", "gz")
    return jax.shard_map(
        body,
        mesh=mesh,
        in_specs=(cells, pair, pair, cells, cells, cells, cells, cells),
        out_specs=P(None, AXES, None),
        check_vma=False,
    )
```

```python
import jax
import jax.numpy as jnp
from jax import lax
from jax.experimental import pallas as pl
from jax.experimental.pallas import tpu as pltpu
from jax.sharding import PartitionSpec as P

AXES = ("gx", "gy", "gz")
F32 = jnp.float32
T = 32
L = 128
H = 10
OJ = 12
EI = T + 2 * H
EJ = 56
SWEEPS = 9
SLOTS = 640
ZG = 10
NQ = 5
SOLVE_MIB = 42
PAD = 8
ZS = 12


def strip_offsets():
    offsets, at = {}, 0
    for side in (0, 1):
        for dist in range(1, H):
            offsets[side, dist] = at
            at += H - dist
    return offsets


STRIPS = strip_offsets()


def plane_of(side, dist):
    return H - dist if side == 0 else dist - 1


def prep_kernel(p, sat, perm, sto, mask, own, xm, xp, ym, yp):
    def rows(q, carry):
        for u in range(4):
            i = q * 4 + u
            act = mask[i].astype(F32)
            s_w, s_g = sat[0, i], sat[1, i]
            s_o = 1.0 - s_w - s_g
            m_w, m_o, m_g = s_w * s_w * 2.0, s_o * s_o * 0.5, s_g * s_g * 4.0
            lam = m_w + m_o + m_g
            cond = perm[i] * act
            diag = act * (sto[i] * (0.5 * s_w + s_o + 2.0 * s_g)) + 3.0 * (1.0 - act)
            a_w, a_g = m_w / lam, m_g / lam
            for f, v in enumerate((cond, lam, diag, a_w, a_g)):
                own[f, i] = v
            for f, v in enumerate((p[i], cond, lam, diag)):
                ym[f * 8 + q, 10 * u : 10 * u + 10] = v[:H]
                yp[f * 8 + q, 10 * u : 10 * u + 10] = v[T - H :]
            for f, v in enumerate((a_w, a_g)):
                ym[32 + f, pl.ds(i, 1)] = v[:1]
                yp[32 + f, pl.ds(i, 1)] = v[T - 1 :]
        return carry

    lax.fori_loop(0, 8, rows, 0)
    for f in range(4):
        for t in range(H):
            xm[f * H + t] = p[t] if f == 0 else own[f - 1, t]
            xp[f * H + t] = p[T - H + t] if f == 0 else own[f - 1, T - H + t]
    for f in range(2):
        xm[4 * H + f] = own[3 + f, 0]
        xp[4 * H + f] = own[3 + f, T - 1]


def strip_kernel(dst, x_lo, x_hi, places, cm, cp):
    del dst, places
    for f in range(4):
        for side, src in ((0, x_lo), (1, x_hi)):
            for dist in range(1, H):
                n, at = H - dist, STRIPS[side, dist]
                t = f * H + plane_of(side, dist)
                cm[f, at : at + n] = src[t, :n]
                cp[f, at : at + n] = src[t, T - n :]


def lanes_of(rows):
    return lax.broadcasted_iota(jnp.int32, (rows, L), 1)


def up(v):
    return pltpu.roll(v, v.shape[0] - 1, 0)


def down(v):
    return pltpu.roll(v, 1, 0)


def turn(v, by):
    return pltpu.roll(v, by % L if isinstance(by, int) else lax.rem(by + 2 * L, L), 1)


def build_kernel(edge, p, own, x_lo, x_hi, y_lo, y_hi, c_lo, c_hi, ext, aext, zm, zp):
    def cells(q, carry):
        for u in range(4):
            i = q * 4 + u
            for f in range(4):
                lo = y_lo[f * 8 + q, 10 * u : 10 * u + 10]
                hi = y_hi[f * 8 + q, 10 * u : 10 * u + 10]
                if f == 1:
                    lo, hi = lo * edge[2], hi * edge[3]
                ext[f, H + i, OJ - H : OJ] = lo
                ext[f, H + i, OJ : OJ + T] = p[i] if f == 0 else own[f - 1, i]
                ext[f, H + i, OJ + T : OJ + T + H] = hi
            for f in range(2):
                aext[f, 1 + i, OJ - 1 : OJ] = y_lo[32 + f, pl.ds(i, 1)]
                aext[f, 1 + i, OJ : OJ + T] = own[3 + f, i]
                aext[f, 1 + i, OJ + T : OJ + T + 1] = y_hi[32 + f, pl.ds(i, 1)]
        return carry

    lax.fori_loop(0, 8, cells, 0)
    for f in range(4):
        for side, src in ((0, x_lo), (1, x_hi)):
            for dist in range(1, H + 1):
                t = plane_of(side, dist)
                i = t if side == 0 else H + T + t
                v = src[f * H + t]
                if f == 1:
                    v = v * edge[side]
                ext[f, i, OJ : OJ + T] = v
                n = H - dist
                if n:
                    at = STRIPS[side, dist]
                    lo, hi = c_lo[f, at : at + n], c_hi[f, at : at + n]
                    if f == 1:
                        lo, hi = lo * (edge[side] * edge[2]), hi * (edge[side] * edge[3])
                    ext[f, i, OJ - n : OJ] = lo
                    ext[f, i, OJ + T : OJ + T + n] = hi
    for f in range(2):
        aext[f, 0, OJ : OJ + T] = x_lo[4 * H + f]
        aext[f, T + 1, OJ : OJ + T] = x_hi[4 * H + f]
    lane = lanes_of(EJ)

    def pack(s, carry):
        f, q = s // NQ, s % NQ
        low = jnp.zeros((EJ, L), F32)
        high = low
        for g in range(ZG):
            i = 1 + q + NQ * g
            r = ext[f, i, :EJ]
            if g:
                r = turn(r, ZS * g)
                ext[f, i, :EJ] = r
            low = jnp.where((lane >= ZS * g) & (lane < ZS * g + H), r, low)
            first = (ZS * g - H) % L
            high = jnp.where((lane >= first) & (lane < first + H), r, high)
        zm[s] = low
        zp[s] = high
        return carry

    lax.fori_loop(0, 4 * NQ, pack, 0)
    for f in range(3):
        ext[f, EI - 1, :EJ] = turn(ext[f, EI - 1, :EJ], ZS * ZG)

    def pack_share(f, carry):
        low = jnp.zeros((EJ, L), F32)
        high = low
        for i in range(T + 2):
            v = aext[f, i]
            if 1 <= i <= T:
                spot = 2 * (i - 1)
                r = turn(v, spot) if spot else v
                low = jnp.where(lane == spot, r, low)
                high = jnp.where(lane == (spot + L - 1) % L, r, high)
            aext[f, i] = turn(v, ZS * ((i + H - 2) // NQ))
        zm[4 * NQ + f] = low
        zp[4 * NQ + f] = high
        return carry

    lax.fori_loop(0, 2, pack_share, 0)


def face(p, c, m, pn, cn, mn):
    trans = 2.0 * c * cn / jnp.maximum(c + cn, 0.5)
    there = trans * jnp.where(p >= pn, m, mn)
    back = trans * jnp.where(pn >= p, mn, m)
    step = pn - p
    return there, back, there * step, back * step


def solve_kernel(
    edge, dst, ext, aext, z_lo, z_hi, z_first, z_last, sat, old, sto, mask, places, send,
    side, rim, back, mat, zmat, base, one, two, zbase, zone, ztwo, border, total, share, spare, rows, stage, sem,
):
    lane = lanes_of(EJ)
    part = lax.rem(lane, ZS)
    first_lane = part == 0
    last_lane = (part == ZS - 1) & (lane < ZS * (ZG - 1)) | (lane == L - 1)
    body_rows = slice(PAD, PAD + EJ)

    def wrap(ref, t):
        ref[t, 0] = turn(ref[t, NQ], ZS)
        ref[t, NQ + 1] = turn(ref[t, 1], -ZS)

    def join(q, carry):
        for f in range(4):
            right, left = z_hi[f * NQ + q], z_lo[f * NQ + q]
            if f == 1:
                right, left = right * edge[5], left * edge[4]
            if f < 3:
                right = jnp.where(last_lane, z_last[f * NQ + q], right)
                left = jnp.where(first_lane, z_first[f * NQ + q], left)
                rim[f, q] = jnp.where(first_lane, z_hi[f * NQ + q], z_lo[f * NQ + q])
                if f == 1:
                    rim[f, q] = jnp.where(first_lane, right, left)
            side[f, 0, 1 + q] = right
            side[f, 1, 1 + q] = left
        return carry

    lax.fori_loop(0, NQ, join, 0)
    for f in range(3):
        for t in (0, 1):
            wrap(side.at[f], t)

    def combine(diag, x, x_carry, y, z, z_back, z_bflow):
        y_back, y_bflow = down(y[1]), down(y[3])
        whole = diag + (x[0] + x_carry[0]) + (y[0] + y_back) + (z[0] + z_back)
        flow = (x[2] - x_carry[1]) + (y[2] - y_bflow) + (z[2] - z_bflow)
        inv = 1.0 / whole
        weights = [w * inv for w in (x[0], x_carry[0], y[0], y_back, z[0], z_back)]
        return whole, flow * inv, weights

    for t in (0, 1):

        def packed(q, carry, t=t):
            here = [side[f, t, q] for f in range(3)]
            x = face(*here, *(side[f, t, q + 1] for f in range(3)))
            y = face(*here, *(up(v) for v in here))
            z = face(*here, *(turn(v, -1) for v in here))
            if t == 1:
                back[0, q - 1] = z[1]
                back[1, q - 1] = z[3]
            _, start, weights = combine(
                side[3, t, q], x, carry, y, z, turn(z[1], 1), turn(z[3], 1)
            )
            for k, w in enumerate(weights):
                zmat[k, t, q - 1] = w
            zbase[t, q, body_rows] = start
            return x[1], x[3]

        x = face(*(side[f, t, 0] for f in range(3)), *(side[f, t, 1] for f in range(3)))
        lax.fori_loop(1, NQ + 1, packed, (x[1], x[3]))

    def spots(g, lanes):
        return lanes == ZS * g, lanes == lax.rem(ZS * g + L - 1, L)

    def ghosts(ref, q, value, rows_at, marks):
        pltpu.store(ref.at[0, 1 + q, rows_at], value, mask=marks[1])
        pltpu.store(ref.at[1, 1 + q, rows_at], value, mask=marks[0])

    all_rows = slice(0, EJ)

    def assemble(g, carry):
        marks = spots(g, lane)
        for q in range(NQ):
            i = 1 + NQ * g + q
            here = [ext[f, i, all_rows] for f in range(3)]
            ahead = [ext[f, i + 1, all_rows] for f in range(3)]
            if q == NQ - 1:
                ahead = [turn(v, -ZS) for v in ahead]
            x = face(*here, *ahead)
            y = face(*here, *(ext[f, i, 1 : EJ + 1] for f in range(3)))
            z = face(
                *here,
                *(turn(jnp.where(marks[0], rim[f, q], v), -1) for f, v in enumerate(here)),
            )
            z_back, z_bflow = (
                turn(jnp.where(marks[1], back[k, q], z[n]), 1) for k, n in ((0, 1), (1, 3))
            )
            whole, start, weights = combine(ext[3, i, all_rows], x, carry, y, z, z_back, z_bflow)
            for k, w in enumerate(weights):
                mat[k, i] = w
            total[i] = whole
            base[i, body_rows] = start
            ghosts(zbase, q, start, body_rows, marks)
            carry = x[1], x[3]
        return tuple(turn(v, ZS) for v in carry)

    x = face(*(ext[f, 0, all_rows] for f in range(3)), *(ext[f, 1, all_rows] for f in range(3)))
    lax.fori_loop(0, ZG, assemble, (x[1], x[3]))

    def prepare(zsrc):
        for t in (0, 1):
            wrap(zsrc, t)

        def plane(q, carry):
            border[q] = jnp.where(
                first_lane, zsrc[0, 1 + q, body_rows], zsrc[1, 1 + q, body_rows]
            )
            return carry

        lax.fori_loop(0, NQ, plane, 0)

    def sweep(src, zsrc, target, ztarget, depth):
        low, high = (0, EJ) if depth > 3 else (8, 48)
        at = slice(low, high)
        y_at = slice(PAD + low, PAD + high)
        y_up, y_down = (slice(y_at.start + k, y_at.stop + k) for k in (1, -1))
        lanes = lane[at]
        prepare(zsrc)

        def halo(q, carry):
            for t in (0, 1):
                y = zsrc[t, q, y_at]
                acc = zbase[t, q, y_at] + zmat[0, t, q - 1, at] * zsrc[t, q + 1, y_at]
                acc = acc + zmat[1, t, q - 1, at] * zsrc[t, q - 1, y_at]
                acc = acc + zmat[2, t, q - 1, at] * zsrc[t, q, y_up]
                acc = acc + zmat[3, t, q - 1, at] * zsrc[t, q, y_down]
                acc = acc + zmat[4, t, q - 1, at] * turn(y, -1)
                ztarget[t, q, y_at] = acc + zmat[5, t, q - 1, at] * turn(y, 1)
            return carry

        lax.fori_loop(1, NQ + 1, halo, 0)

        def planes(g, carry):
            marks = spots(g, lanes)
            for q in range(NQ):
                i = 1 + NQ * g + q
                y, near = src[i, y_at], border[q, at]
                ahead, behind = src[i + 1, y_at], src[i - 1, y_at]
                if q == 0:
                    behind = turn(behind, ZS)
                if q == NQ - 1:
                    ahead = turn(ahead, -ZS)
                acc = base[i, y_at] + mat[0, i, at] * ahead
                acc = acc + mat[1, i, at] * behind
                acc = acc + mat[2, i, at] * src[i, y_up]
                acc = acc + mat[3, i, at] * src[i, y_down]
                acc = acc + mat[4, i, at] * turn(jnp.where(marks[0], near, y), -1)
                acc = acc + mat[5, i, at] * turn(jnp.where(marks[1], near, y), 1)
                target[i, y_at] = acc
                ghosts(ztarget, q, acc, y_at, marks)
            return carry

        lax.fori_loop(*((0, ZG) if depth > 4 else (1, ZG - 1)), planes, 0)

    src, zsrc = base, zbase
    for k in range(1, SWEEPS):
        target, ztarget = (one, zone) if k % 2 else (two, ztwo)
        sweep(src, zsrc, target, ztarget, SWEEPS - k)
        src, zsrc = target, ztarget
    prepare(zsrc)

    mid, mid_up, mid_down = slice(8, 48), slice(9, 49), slice(7, 47)
    y_mid, y_up, y_down = (slice(PAD + k, PAD + 40 + k) for k in (8, 9, 7))
    lanes = lane[mid]
    even = lax.rem(lanes, 2) == 0
    for f in range(2):
        share[f] = jnp.where(even, z_hi[4 * NQ + f, mid], z_lo[4 * NQ + f, mid])

    def near_of(ref, lead, i, at, at_up, at_down, edge_plane, q, marks):
        here, ahead, behind = (ref[lead + (i + k, at)] for k in (0, 1, -1))
        if q == 0:
            behind = turn(behind, ZS)
        if q == NQ - 1:
            ahead = turn(ahead, -ZS)
        return here, (
            ahead,
            behind,
            ref[lead + (i, at_up)],
            ref[lead + (i, at_down)],
            turn(jnp.where(marks[0], edge_plane, here), -1),
            turn(jnp.where(marks[1], edge_plane, here), 1),
        )

    def finish(g, q, marks):
        e = 1 + NQ * g + q
        i = e - H
        pa, p_near = near_of(ext, (0,), e, mid, mid_up, mid_down, rim[0, q, mid], q, marks)
        _, s_near = near_of(src, (), e, y_mid, y_up, y_down, border[q, mid], q, marks)
        shares = [
            near_of(
                aext, (f,), i + 1, mid, mid_up, mid_down,
                turn(share[f], ZS * g - 2 * i), q, marks,
            )
            for f in range(2)
        ]
        x_p = base[e, y_mid]
        for k in range(6):
            x_p = x_p + mat[k, e, mid] * s_near[k]
        column = [jnp.zeros((40, L), F32) for _ in range(2)]
        drive = [jnp.zeros((40, L), F32) for _ in range(2)]
        for k in range(6):
            weight = mat[k, e, mid]
            upstream = pa >= p_near[k]
            step = s_near[k] - (pa - p_near[k])
            for f, (a, a_near) in enumerate(shares):
                w = weight * jnp.where(upstream, a, a_near[k])
                column[f] = column[f] + w
                drive[f] = drive[f] + w * step
        scale = total[e, mid]
        shift = -ZS * g
        spare[0] = turn(x_p, shift)
        for f in range(2):
            spare[1 + f] = turn((drive[f] - column[f] * x_p) * scale, shift)
        x_p = spare[0, 4:36]
        act = mask[i].astype(F32)
        held = act * sto[i]
        idle = 1.0 - act
        inverse = 1.0 / (held + idle)
        stage[0, i] = x_p
        for f, compress in ((0, 0.5), (1, 2.0)):
            s_now = sat[f, i]
            local = (held * (compress * s_now) + idle) * x_p
            change = held * (s_now - old[f, i])
            stage[1 + f, i] = (spare[1 + f, 4:36] - change - local) * inverse

    def group(g, carry):
        marks = spots(g, lanes)
        for q in range(NQ):
            finish(g, q, marks)
        return carry

    lax.fori_loop(2, 8, group, 0)
    finish(jnp.int32(1), NQ - 1, spots(1, lanes))
    finish(jnp.int32(8), 0, spots(8, lanes))

    devices = places.shape[0]
    capacity = T * T // devices
    chunk = 3 * capacity + 1

    def place(i, carry):
        for j in range(T):
            d = dst[i * T + j]
            for f in range(3):
                rows[pl.ds(d + f * capacity, 1)] = stage[f, i, j : j + 1]
        return carry

    lax.fori_loop(0, T, place, 0)

    def tail(d, carry):
        rows[pl.ds(d * chunk + 3 * capacity, 1)] = places[pl.ds(d, 1)]
        return carry

    lax.fori_loop(0, devices, tail, 0, unroll=8)
    copy = pltpu.make_async_copy(rows.at[: devices * chunk], send, sem)
    copy.start()
    copy.wait()


def index_kernel(owner, slot, dst, place, count):
    devices = count.shape[0]
    capacity = T * T // devices
    chunk = 3 * capacity + 1

    def clear(d, carry):
        count[d] = 0
        return carry

    def blank(d, carry):
        place[d] = -1
        return carry

    lax.fori_loop(0, devices, clear, 0)
    lax.fori_loop(0, T * T, blank, 0, unroll=8)

    def row(r, carry):
        o = owner[r]

        @pl.when(o >= 0)
        def _():
            n = count[o]
            count[o] = n + 1
            place[o * capacity + n] = slot[r]
            dst[r] = o * chunk + n

        @pl.when(o < 0)
        def _():
            dst[r] = devices * chunk

        return carry

    lax.fori_loop(0, T * T, row, 0)


def unpack_kernel(got, update, held, number, table, where, sem):
    devices = where.shape[0]
    capacity = T * T // devices
    chunk = 3 * capacity + 1

    def collect(d, carry):
        number[pl.ds(d, 1)] = got[pl.ds(d * chunk + 3 * capacity, 1)]
        return carry

    lax.fori_loop(0, devices, collect, 0, unroll=8)
    slots = number[...].astype(jnp.int32)
    table[...] = jnp.where(slots < 0, SLOTS, slots)
    copy = pltpu.make_async_copy(table, where, sem)
    copy.start()
    copy.wait()

    def scatter(d, carry):
        for k in range(capacity):
            s = where[d, k]
            for f in range(3):
                held[f, pl.ds(s, 1)] = got[pl.ds(d * chunk + f * capacity + k, 1)]
        return carry

    lax.fori_loop(0, devices, scatter, 0)
    copy = pltpu.make_async_copy(held.at[:, :SLOTS], update, sem)
    copy.start()
    copy.wait()


def spec(space):
    return pl.BlockSpec(memory_space=space)


def shape(*dims):
    return jax.ShapeDtypeStruct(dims, F32)


def call(kernel, name, out_shape, smem, count, out_spaces=None, scratch=(), limit=16):
    many = isinstance(out_shape, (tuple, list))
    spaces = out_spaces or ([pltpu.VMEM] * len(out_shape) if many else pltpu.VMEM)
    return pl.pallas_call(
        kernel,
        name=name,
        out_shape=out_shape,
        in_specs=[spec(pltpu.SMEM)] * smem + [spec(pltpu.VMEM)] * count,
        out_specs=[spec(s) for s in spaces] if many else spec(spaces),
        scratch_shapes=list(scratch),
        compiler_params=pltpu.CompilerParams(vmem_limit_bytes=limit << 20),
    )


def ring(axis, step):
    size = lax.axis_size(axis)
    return [(i, (i + step) % size) for i in range(size)]


def swap(low, high, axis):
    return lax.ppermute(high, axis, ring(axis, 1)), lax.ppermute(low, axis, ring(axis, -1))


def body(
    pressure, saturation, old_saturation, permeability, storage, cell_mask, row_owner, row_slot
):
    devices = lax.axis_size(AXES)
    capacity = T * T // devices
    chunk = 3 * capacity + 1
    inside = []
    for axis in AXES:
        at = lax.axis_index(axis)
        inside += [at > 0, at < lax.axis_size(axis) - 1]
    edge = jnp.stack(inside).astype(F32)

    own, xm, xp, ym, yp = call(
        prep_kernel,
        "prep",
        (
            shape(5, T, T, L),
            shape(4 * H + 2, T, L),
            shape(4 * H + 2, T, L),
            shape(34, 40, L),
            shape(34, 40, L),
        ),
        0,
        5,
    )(pressure, saturation, permeability, storage, cell_mask)
    x_lo, x_hi = swap(xm, xp, "gx")
    y_lo, y_hi = swap(ym, yp, "gy")

    ints = jax.ShapeDtypeStruct((T * T,), jnp.int32)
    dst, place = call(
        index_kernel,
        "index",
        (ints, ints),
        2,
        0,
        [pltpu.SMEM] * 2,
        [pltpu.SMEM((devices,), jnp.int32)],
    )(row_owner.reshape(T * T), row_slot.reshape(T * T))
    places = jnp.pad(
        place.reshape(devices, capacity).astype(F32), ((0, 0), (0, L - capacity))
    )

    cm, cp = call(strip_kernel, "strip", (shape(4, 96, L), shape(4, 96, L)), 1, 3)(
        dst, x_lo, x_hi, places
    )
    c_lo, c_hi = swap(cm, cp, "gy")
    ext, aext, zm, zp = call(
        build_kernel,
        "build",
        (shape(4, EI, EJ + 8, L), shape(2, T + 2, EJ, L), shape(22, EJ, L), shape(22, EJ, L)),
        1,
        8,
        limit=24,
    )(edge, pressure, own, x_lo, x_hi, y_lo, y_hi, c_lo, c_hi)
    z_lo, z_hi = swap(zm, zp, "gz")
    send = call(
        solve_kernel,
        "solve",
        shape(devices * chunk, L),
        2,
        11,
        pl.ANY,
        [
            pltpu.VMEM((4, 2, NQ + 2, EJ, L), F32),
            pltpu.VMEM((3, NQ, EJ, L), F32),
            pltpu.VMEM((2, NQ, EJ, L), F32),
            pltpu.VMEM((6, EI, EJ, L), F32),
            pltpu.VMEM((6, 2, NQ, EJ, L), F32),
        ]
        + [pltpu.VMEM((EI, EJ + 2 * PAD, L), F32)] * 3
        + [pltpu.VMEM((2, NQ + 2, EJ + 2 * PAD, L), F32)] * 3
        + [
            pltpu.VMEM((NQ, EJ, L), F32),
            pltpu.VMEM((EI, EJ, L), F32),
            pltpu.VMEM((2, 40, L), F32),
            pltpu.VMEM((3, 40, L), F32),
            pltpu.VMEM((devices * chunk + 2 * capacity + 8, L), F32),
            pltpu.VMEM((3, T, T, L), F32),
            pltpu.SemaphoreType.DMA(()),
        ],
        SOLVE_MIB,
    )(
        edge, dst, ext, aext, z_lo, z_hi, zm, zp,
        saturation, old_saturation, storage, cell_mask, places,
    )
    got = lax.all_to_all(
        send.reshape(devices, chunk, 1, L), AXES, split_axis=0, concat_axis=0, tiled=True
    )
    return call(
        unpack_kernel,
        "unpack",
        shape(3, SLOTS, L),
        0,
        1,
        pl.ANY,
        [
            pltpu.VMEM((3, SLOTS + 8, L), F32),
            pltpu.VMEM((devices, L), F32),
            pltpu.VMEM((devices, L), jnp.int32),
            pltpu.SMEM((devices, L), jnp.int32),
            pltpu.SemaphoreType.DMA(()),
        ],
    )(got.reshape(devices * chunk, L))


def solution(mesh):
    cells = P("gx", "gy", "gz")
    pair = P(None, "gx", "gy", "gz")
    return jax.shard_map(
        body,
        mesh=mesh,
        in_specs=(cells, pair, pair, cells, cells, cells, cells, cells),
        out_specs=P(None, AXES, None),
        check_vma=False,
    )
```

```python
import jax
import jax.numpy as jnp
from jax import lax
from jax.experimental import pallas as pl
from jax.experimental.pallas import tpu as pltpu
from jax.sharding import PartitionSpec as P

AXES = ("gx", "gy", "gz")
F32 = jnp.float32
T = 32
L = 128
H = 10
OJ = 12
EI = T + 2 * H
EJ = 56
SWEEPS = 9
SLOTS = 640
ZG = 10
NQ = 5
SOLVE_MIB = 34
PAD = 8
ZS = 12


def strip_offsets():
    offsets, at = {}, 0
    for side in (0, 1):
        for dist in range(1, H):
            offsets[side, dist] = at
            at += H - dist
    return offsets


STRIPS = strip_offsets()


def plane_of(side, dist):
    return H - dist if side == 0 else dist - 1


def prep_kernel(p, sat, perm, sto, mask, own, xm, xp, ym, yp):
    def rows(q, carry):
        for u in range(4):
            i = q * 4 + u
            act = mask[i].astype(F32)
            s_w, s_g = sat[0, i], sat[1, i]
            s_o = 1.0 - s_w - s_g
            m_w, m_o, m_g = s_w * s_w * 2.0, s_o * s_o * 0.5, s_g * s_g * 4.0
            lam = m_w + m_o + m_g
            cond = perm[i] * act
            diag = act * (sto[i] * (0.5 * s_w + s_o + 2.0 * s_g)) + 3.0 * (1.0 - act)
            a_w, a_g = m_w / lam, m_g / lam
            for f, v in enumerate((cond, lam, diag, a_w, a_g)):
                own[f, i] = v
            for f, v in enumerate((p[i], cond, lam, diag)):
                ym[f * 8 + q, 10 * u : 10 * u + 10] = v[:H]
                yp[f * 8 + q, 10 * u : 10 * u + 10] = v[T - H :]
            for f, v in enumerate((a_w, a_g)):
                ym[32 + f, pl.ds(i, 1)] = v[:1]
                yp[32 + f, pl.ds(i, 1)] = v[T - 1 :]
        return carry

    lax.fori_loop(0, 8, rows, 0)
    for f in range(4):
        for t in range(H):
            xm[f * H + t] = p[t] if f == 0 else own[f - 1, t]
            xp[f * H + t] = p[T - H + t] if f == 0 else own[f - 1, T - H + t]
    for f in range(2):
        xm[4 * H + f] = own[3 + f, 0]
        xp[4 * H + f] = own[3 + f, T - 1]


def strip_kernel(dst, x_lo, x_hi, places, cm, cp):
    del dst, places
    for f in range(4):
        for side, src in ((0, x_lo), (1, x_hi)):
            for dist in range(1, H):
                n, at = H - dist, STRIPS[side, dist]
                t = f * H + plane_of(side, dist)
                cm[f, at : at + n] = src[t, :n]
                cp[f, at : at + n] = src[t, T - n :]


def lanes_of(rows):
    return lax.broadcasted_iota(jnp.int32, (rows, L), 1)


def up(v):
    return pltpu.roll(v, v.shape[0] - 1, 0)


def down(v):
    return pltpu.roll(v, 1, 0)


def turn(v, by):
    return pltpu.roll(v, by % L if isinstance(by, int) else lax.rem(by + 2 * L, L), 1)


def build_kernel(edge, p, own, x_lo, x_hi, y_lo, y_hi, c_lo, c_hi, ext, aext, zm, zp):
    def cells(q, carry):
        for u in range(4):
            i = q * 4 + u
            for f in range(4):
                lo = y_lo[f * 8 + q, 10 * u : 10 * u + 10]
                hi = y_hi[f * 8 + q, 10 * u : 10 * u + 10]
                if f == 1:
                    lo, hi = lo * edge[2], hi * edge[3]
                ext[f, H + i, OJ - H : OJ] = lo
                ext[f, H + i, OJ : OJ + T] = p[i] if f == 0 else own[f - 1, i]
                ext[f, H + i, OJ + T : OJ + T + H] = hi
            for f in range(2):
                aext[f, 1 + i, OJ - 1 : OJ] = y_lo[32 + f, pl.ds(i, 1)]
                aext[f, 1 + i, OJ : OJ + T] = own[3 + f, i]
                aext[f, 1 + i, OJ + T : OJ + T + 1] = y_hi[32 + f, pl.ds(i, 1)]
        return carry

    lax.fori_loop(0, 8, cells, 0)
    for f in range(4):
        for side, src in ((0, x_lo), (1, x_hi)):
            for dist in range(1, H + 1):
                t = plane_of(side, dist)
                i = t if side == 0 else H + T + t
                v = src[f * H + t]
                if f == 1:
                    v = v * edge[side]
                ext[f, i, OJ : OJ + T] = v
                n = H - dist
                if n:
                    at = STRIPS[side, dist]
                    lo, hi = c_lo[f, at : at + n], c_hi[f, at : at + n]
                    if f == 1:
                        lo, hi = lo * (edge[side] * edge[2]), hi * (edge[side] * edge[3])
                    ext[f, i, OJ - n : OJ] = lo
                    ext[f, i, OJ + T : OJ + T + n] = hi
    for f in range(2):
        aext[f, 0, OJ : OJ + T] = x_lo[4 * H + f]
        aext[f, T + 1, OJ : OJ + T] = x_hi[4 * H + f]
    lane = lanes_of(EJ)

    def pack(s, carry):
        f, q = s // NQ, s % NQ
        low = jnp.zeros((EJ, L), F32)
        high = low
        for g in range(ZG):
            i = 1 + q + NQ * g
            r = ext[f, i, :EJ]
            if g:
                r = turn(r, ZS * g)
                ext[f, i, :EJ] = r
            low = jnp.where((lane >= ZS * g) & (lane < ZS * g + H), r, low)
            first = (ZS * g - H) % L
            high = jnp.where((lane >= first) & (lane < first + H), r, high)
        zm[s] = low
        zp[s] = high
        return carry

    lax.fori_loop(0, 4 * NQ, pack, 0)
    for f in range(3):
        ext[f, EI - 1, :EJ] = turn(ext[f, EI - 1, :EJ], ZS * ZG)

    def pack_share(f, carry):
        low = jnp.zeros((EJ, L), F32)
        high = low
        for i in range(T + 2):
            v = aext[f, i]
            if 1 <= i <= T:
                spot = 2 * (i - 1)
                r = turn(v, spot) if spot else v
                low = jnp.where(lane == spot, r, low)
                high = jnp.where(lane == (spot + L - 1) % L, r, high)
            aext[f, i] = turn(v, ZS * ((i + H - 2) // NQ))
        zm[4 * NQ + f] = low
        zp[4 * NQ + f] = high
        return carry

    lax.fori_loop(0, 2, pack_share, 0)


def face(p, c, m, pn, cn, mn):
    trans = 2.0 * c * cn / jnp.maximum(c + cn, 0.5)
    there = trans * jnp.where(p >= pn, m, mn)
    back = trans * jnp.where(pn >= p, mn, m)
    step = pn - p
    return there, back, there * step, back * step


def solve_kernel(
    edge, dst, ext, aext, z_lo, z_hi, z_first, z_last, sat, old, sto, mask, places, send,
    side, rim, back, mat, zmat, base, one, two, zbase, zone, ztwo, border, total, share, rows, stage, sem,
):
    lane = lanes_of(EJ)
    part = lax.rem(lane, ZS)
    first_lane = part == 0
    last_lane = (part == ZS - 1) & (lane < ZS * (ZG - 1)) | (lane == L - 1)
    body_rows = slice(PAD, PAD + EJ)

    def wrap(ref, t):
        ref[t, 0] = turn(ref[t, NQ], ZS)
        ref[t, NQ + 1] = turn(ref[t, 1], -ZS)

    def join(q, carry):
        for f in range(4):
            right, left = z_hi[f * NQ + q], z_lo[f * NQ + q]
            if f == 1:
                right, left = right * edge[5], left * edge[4]
            if f < 3:
                right = jnp.where(last_lane, z_last[f * NQ + q], right)
                left = jnp.where(first_lane, z_first[f * NQ + q], left)
                rim[f, q] = jnp.where(first_lane, z_hi[f * NQ + q], z_lo[f * NQ + q])
                if f == 1:
                    rim[f, q] = jnp.where(first_lane, right, left)
            side[f, 0, 1 + q] = right
            side[f, 1, 1 + q] = left
        return carry

    lax.fori_loop(0, NQ, join, 0)
    for f in range(3):
        for t in (0, 1):
            wrap(side.at[f], t)

    def combine(diag, x, x_carry, y, z, z_back, z_bflow):
        y_back, y_bflow = down(y[1]), down(y[3])
        whole = diag + (x[0] + x_carry[0]) + (y[0] + y_back) + (z[0] + z_back)
        flow = (x[2] - x_carry[1]) + (y[2] - y_bflow) + (z[2] - z_bflow)
        inv = 1.0 / whole
        weights = [w * inv for w in (x[0], x_carry[0], y[0], y_back, z[0], z_back)]
        return whole, flow * inv, weights

    for t in (0, 1):

        def packed(q, carry, t=t):
            here = [side[f, t, q] for f in range(3)]
            x = face(*here, *(side[f, t, q + 1] for f in range(3)))
            y = face(*here, *(up(v) for v in here))
            z = face(*here, *(turn(v, -1) for v in here))
            if t == 1:
                back[0, q - 1] = z[1]
                back[1, q - 1] = z[3]
            _, start, weights = combine(
                side[3, t, q], x, carry, y, z, turn(z[1], 1), turn(z[3], 1)
            )
            for k, w in enumerate(weights):
                zmat[k, t, q - 1] = w
            zbase[t, q, body_rows] = start
            return x[1], x[3]

        x = face(*(side[f, t, 0] for f in range(3)), *(side[f, t, 1] for f in range(3)))
        lax.fori_loop(1, NQ + 1, packed, (x[1], x[3]))

    def spots(g, lanes):
        return lanes == ZS * g, lanes == lax.rem(ZS * g + L - 1, L)

    def ghosts(ref, q, value, rows_at, marks):
        pltpu.store(ref.at[0, 1 + q, rows_at], value, mask=marks[1])
        pltpu.store(ref.at[1, 1 + q, rows_at], value, mask=marks[0])

    all_rows = slice(0, EJ)

    def assemble(g, carry):
        marks = spots(g, lane)
        for q in range(NQ):
            i = 1 + NQ * g + q
            here = [ext[f, i, all_rows] for f in range(3)]
            ahead = [ext[f, i + 1, all_rows] for f in range(3)]
            if q == NQ - 1:
                ahead = [turn(v, -ZS) for v in ahead]
            x = face(*here, *ahead)
            y = face(*here, *(ext[f, i, 1 : EJ + 1] for f in range(3)))
            z = face(
                *here,
                *(turn(jnp.where(marks[0], rim[f, q], v), -1) for f, v in enumerate(here)),
            )
            z_back, z_bflow = (
                turn(jnp.where(marks[1], back[k, q], z[n]), 1) for k, n in ((0, 1), (1, 3))
            )
            whole, start, weights = combine(ext[3, i, all_rows], x, carry, y, z, z_back, z_bflow)
            for k, w in enumerate(weights):
                mat[k, i] = w
            total[i] = whole
            base[i, body_rows] = start
            ghosts(zbase, q, start, body_rows, marks)
            carry = x[1], x[3]
        return tuple(turn(v, ZS) for v in carry)

    x = face(*(ext[f, 0, all_rows] for f in range(3)), *(ext[f, 1, all_rows] for f in range(3)))
    lax.fori_loop(0, ZG, assemble, (x[1], x[3]))

    def prepare(zsrc):
        for t in (0, 1):
            wrap(zsrc, t)

        def plane(q, carry):
            border[q] = jnp.where(
                first_lane, zsrc[0, 1 + q, body_rows], zsrc[1, 1 + q, body_rows]
            )
            return carry

        lax.fori_loop(0, NQ, plane, 0)

    def sweep(src, zsrc, target, ztarget, depth):
        low, high = (4, 52) if depth > 4 else (8, 48)
        at = slice(low, high)
        y_at = slice(PAD + low, PAD + high)
        y_up, y_down = (slice(y_at.start + k, y_at.stop + k) for k in (1, -1))
        lanes = lanes_of(high - low)
        prepare(zsrc)

        def halo(q, carry):
            for t in (0, 1):
                y = zsrc[t, q, y_at]
                acc = zbase[t, q, y_at] + zmat[0, t, q - 1, at] * zsrc[t, q + 1, y_at]
                acc = acc + zmat[1, t, q - 1, at] * zsrc[t, q - 1, y_at]
                acc = acc + zmat[2, t, q - 1, at] * zsrc[t, q, y_up]
                acc = acc + zmat[3, t, q - 1, at] * zsrc[t, q, y_down]
                acc = acc + zmat[4, t, q - 1, at] * turn(y, -1)
                ztarget[t, q, y_at] = acc + zmat[5, t, q - 1, at] * turn(y, 1)
            return carry

        lax.fori_loop(1, NQ + 1, halo, 0)

        def planes(g, carry):
            marks = spots(g, lanes)
            for q in range(NQ):
                i = 1 + NQ * g + q
                y, near = src[i, y_at], border[q, at]
                ahead, behind = src[i + 1, y_at], src[i - 1, y_at]
                if q == 0:
                    behind = turn(behind, ZS)
                if q == NQ - 1:
                    ahead = turn(ahead, -ZS)
                acc = base[i, y_at] + mat[0, i, at] * ahead
                acc = acc + mat[1, i, at] * behind
                acc = acc + mat[2, i, at] * src[i, y_up]
                acc = acc + mat[3, i, at] * src[i, y_down]
                acc = acc + mat[4, i, at] * turn(jnp.where(marks[0], near, y), -1)
                acc = acc + mat[5, i, at] * turn(jnp.where(marks[1], near, y), 1)
                target[i, y_at] = acc
                ghosts(ztarget, q, acc, y_at, marks)
            return carry

        lax.fori_loop(*((0, ZG) if depth > 4 else (1, ZG - 1)), planes, 0)

    src, zsrc = base, zbase
    for k in range(1, SWEEPS):
        target, ztarget = (one, zone) if k % 2 else (two, ztwo)
        sweep(src, zsrc, target, ztarget, SWEEPS - k)
        src, zsrc = target, ztarget
    prepare(zsrc)

    mid, mid_up, mid_down = (slice(k, k + T) for k in (OJ, OJ + 1, OJ - 1))
    y_mid, y_up, y_down = (slice(PAD + k, PAD + k + T) for k in (OJ, OJ + 1, OJ - 1))
    lanes = lanes_of(T)
    even = lax.rem(lanes, 2) == 0
    for f in range(2):
        share[f] = jnp.where(even, z_hi[4 * NQ + f, mid], z_lo[4 * NQ + f, mid])

    def near_of(ref, lead, i, at, at_up, at_down, edge_plane, q, marks):
        here, ahead, behind = (ref[lead + (i + k, at)] for k in (0, 1, -1))
        if q == 0:
            behind = turn(behind, ZS)
        if q == NQ - 1:
            ahead = turn(ahead, -ZS)
        return here, (
            ahead,
            behind,
            ref[lead + (i, at_up)],
            ref[lead + (i, at_down)],
            turn(jnp.where(marks[0], edge_plane, here), -1),
            turn(jnp.where(marks[1], edge_plane, here), 1),
        )

    def finish(g, q, marks):
        e = 1 + NQ * g + q
        i = e - H
        pa, p_near = near_of(ext, (0,), e, mid, mid_up, mid_down, rim[0, q, mid], q, marks)
        _, s_near = near_of(src, (), e, y_mid, y_up, y_down, border[q, mid], q, marks)
        shares = [
            near_of(
                aext, (f,), i + 1, mid, mid_up, mid_down,
                turn(share[f], ZS * g - 2 * i), q, marks,
            )
            for f in range(2)
        ]
        x_p = base[e, y_mid]
        for k in range(6):
            x_p = x_p + mat[k, e, mid] * s_near[k]
        column = [jnp.zeros((T, L), F32) for _ in range(2)]
        drive = [jnp.zeros((T, L), F32) for _ in range(2)]
        for k in range(6):
            weight = mat[k, e, mid]
            upstream = pa >= p_near[k]
            step = s_near[k] - (pa - p_near[k])
            for f, (a, a_near) in enumerate(shares):
                w = weight * jnp.where(upstream, a, a_near[k])
                column[f] = column[f] + w
                drive[f] = drive[f] + w * step
        scale = total[e, mid]
        shift = -ZS * g
        coupled = [turn((drive[f] - column[f] * x_p) * scale, shift) for f in range(2)]
        x_p = turn(x_p, shift)
        act = mask[i].astype(F32)
        held = act * sto[i]
        idle = 1.0 - act
        inverse = 1.0 / (held + idle)
        stage[0, i] = x_p
        for f, compress in ((0, 0.5), (1, 2.0)):
            s_now = sat[f, i]
            local = (held * (compress * s_now) + idle) * x_p
            change = held * (s_now - old[f, i])
            stage[1 + f, i] = (coupled[f] - change - local) * inverse

    def group(g, carry):
        marks = spots(g, lanes)
        for q in range(NQ):
            finish(g, q, marks)
        return carry

    lax.fori_loop(2, 8, group, 0)
    finish(jnp.int32(1), NQ - 1, spots(1, lanes))
    finish(jnp.int32(8), 0, spots(8, lanes))

    devices = places.shape[0]
    capacity = T * T // devices
    chunk = 3 * capacity + 1

    def place(i, carry):
        for j in range(T):
            d = dst[i * T + j]
            for f in range(3):
                rows[pl.ds(d + f * capacity, 1)] = stage[f, i, j : j + 1]
        return carry

    lax.fori_loop(0, T, place, 0)

    def tail(d, carry):
        rows[pl.ds(d * chunk + 3 * capacity, 1)] = places[pl.ds(d, 1)]
        return carry

    lax.fori_loop(0, devices, tail, 0, unroll=8)
    copy = pltpu.make_async_copy(rows.at[: devices * chunk], send, sem)
    copy.start()
    copy.wait()


def index_kernel(owner, slot, dst, places):
    devices = places.shape[0]
    capacity = T * T // devices
    chunk = 3 * capacity + 1
    bf16 = jnp.bfloat16
    who = lax.broadcasted_iota(jnp.int32, (devices, L), 0)
    spot = lax.broadcasted_iota(jnp.int32, (L, L), 0)
    earlier = (spot < lax.broadcasted_iota(jnp.int32, (L, L), 1)).astype(F32).astype(bf16)
    count = jnp.zeros((devices, 1), F32)
    coarse = jnp.zeros((devices, L), F32)
    fine = coarse
    for c in range(T * T // L):
        own = owner[c : c + 1]
        hit = (who == own).astype(F32)
        ahead = jnp.dot(hit.astype(bf16), earlier, preferred_element_type=F32) + count
        count = count + jnp.sum(hit, axis=1, keepdims=True)
        rank = jnp.sum(hit * ahead, axis=0, keepdims=True).astype(jnp.int32)
        dst[c : c + 1] = jnp.where(own >= 0, own * chunk + rank, devices * chunk)
        place = slot[c : c + 1]
        high = lax.div(place, 32)
        here = spot == rank
        for part, value in enumerate((high, place - 32 * high)):
            row = jnp.where(here, value.astype(F32), 0.0).astype(bf16)
            found = lax.dot_general(
                hit.astype(bf16), row, (((1,), (1,)), ((), ())), preferred_element_type=F32
            )
            if part == 0:
                coarse = coarse + found
            else:
                fine = fine + found
    lane = lax.broadcasted_iota(jnp.int32, (devices, L), 1).astype(F32)
    places[...] = jnp.where(lane < count, 32.0 * coarse + fine, -1.0)


def unpack_kernel(got, update, held, number, table, where, sem):
    devices = where.shape[0]
    capacity = T * T // devices
    chunk = 3 * capacity + 1

    def collect(d, carry):
        number[pl.ds(d, 1)] = got[pl.ds(d * chunk + 3 * capacity, 1)]
        return carry

    lax.fori_loop(0, devices, collect, 0, unroll=8)
    slots = number[...].astype(jnp.int32)
    table[...] = jnp.where(slots < 0, SLOTS, slots)
    copy = pltpu.make_async_copy(table, where, sem)
    copy.start()
    copy.wait()

    def scatter(d, carry):
        for k in range(capacity):
            s = where[d, k]
            for f in range(3):
                held[f, pl.ds(s, 1)] = got[pl.ds(d * chunk + f * capacity + k, 1)]
        return carry

    lax.fori_loop(0, devices, scatter, 0)
    copy = pltpu.make_async_copy(held.at[:, :SLOTS], update, sem)
    copy.start()
    copy.wait()


def spec(space):
    return pl.BlockSpec(memory_space=space)


def shape(*dims):
    return jax.ShapeDtypeStruct(dims, F32)


def call(kernel, name, out_shape, smem, count, out_spaces=None, scratch=(), limit=16):
    many = isinstance(out_shape, (tuple, list))
    spaces = out_spaces or ([pltpu.VMEM] * len(out_shape) if many else pltpu.VMEM)
    return pl.pallas_call(
        kernel,
        name=name,
        out_shape=out_shape,
        in_specs=[spec(pltpu.SMEM)] * smem + [spec(pltpu.VMEM)] * count,
        out_specs=[spec(s) for s in spaces] if many else spec(spaces),
        scratch_shapes=list(scratch),
        compiler_params=pltpu.CompilerParams(vmem_limit_bytes=limit << 20),
    )


def ring(axis, step):
    size = lax.axis_size(axis)
    return [(i, (i + step) % size) for i in range(size)]


def swap(low, high, axis):
    return lax.ppermute(high, axis, ring(axis, 1)), lax.ppermute(low, axis, ring(axis, -1))


def body(
    pressure, saturation, old_saturation, permeability, storage, cell_mask, row_owner, row_slot
):
    devices = lax.axis_size(AXES)
    capacity = T * T // devices
    chunk = 3 * capacity + 1
    inside = []
    for axis in AXES:
        at = lax.axis_index(axis)
        inside += [at > 0, at < lax.axis_size(axis) - 1]
    edge = jnp.stack(inside).astype(F32)

    own, xm, xp, ym, yp = call(
        prep_kernel,
        "prep",
        (
            shape(5, T, T, L),
            shape(4 * H + 2, T, L),
            shape(4 * H + 2, T, L),
            shape(34, 40, L),
            shape(34, 40, L),
        ),
        0,
        5,
        limit=60,
    )(pressure, saturation, permeability, storage, cell_mask)
    x_lo, x_hi = swap(xm, xp, "gx")
    y_lo, y_hi = swap(ym, yp, "gy")

    table = (T * T // L, L)
    dst, places = call(
        index_kernel, "index", (jax.ShapeDtypeStruct(table, jnp.int32), shape(devices, L)), 0, 2
    )(row_owner.reshape(table), row_slot.reshape(table))
    dst = dst.reshape(T * T)

    cm, cp = call(strip_kernel, "strip", (shape(4, 96, L), shape(4, 96, L)), 1, 3)(
        dst, x_lo, x_hi, places
    )
    c_lo, c_hi = swap(cm, cp, "gy")
    ext, aext, zm, zp = call(
        build_kernel,
        "build",
        (shape(4, EI, EJ + 8, L), shape(2, T + 2, EJ, L), shape(22, EJ, L), shape(22, EJ, L)),
        1,
        8,
        limit=24,
    )(edge, pressure, own, x_lo, x_hi, y_lo, y_hi, c_lo, c_hi)
    z_lo, z_hi = swap(zm, zp, "gz")
    send = call(
        solve_kernel,
        "solve",
        shape(devices * chunk, L),
        2,
        11,
        pl.ANY,
        [
            pltpu.VMEM((4, 2, NQ + 2, EJ, L), F32),
            pltpu.VMEM((3, NQ, EJ, L), F32),
            pltpu.VMEM((2, NQ, EJ, L), F32),
            pltpu.VMEM((6, EI, EJ, L), F32),
            pltpu.VMEM((6, 2, NQ, EJ, L), F32),
        ]
        + [pltpu.VMEM((EI, EJ + 2 * PAD, L), F32)] * 3
        + [pltpu.VMEM((2, NQ + 2, EJ + 2 * PAD, L), F32)] * 3
        + [
            pltpu.VMEM((NQ, EJ, L), F32),
            pltpu.VMEM((EI, EJ, L), F32),
            pltpu.VMEM((2, T, L), F32),
            pltpu.VMEM((devices * chunk + 2 * capacity + 8, L), F32),
            pltpu.VMEM((3, T, T, L), F32),
            pltpu.SemaphoreType.DMA(()),
        ],
        SOLVE_MIB,
    )(
        edge, dst, ext, aext, z_lo, z_hi, zm, zp,
        saturation, old_saturation, storage, cell_mask, places,
    )
    got = lax.all_to_all(
        send.reshape(devices, chunk, 1, L), AXES, split_axis=0, concat_axis=0, tiled=True
    )
    return call(
        unpack_kernel,
        "unpack",
        shape(3, SLOTS, L),
        0,
        1,
        pl.ANY,
        [
            pltpu.VMEM((3, SLOTS + 8, L), F32),
            pltpu.VMEM((devices, L), F32),
            pltpu.VMEM((devices, L), jnp.int32),
            pltpu.SMEM((devices, L), jnp.int32),
            pltpu.SemaphoreType.DMA(()),
        ],
    )(got.reshape(devices * chunk, L))


def solution(mesh):
    cells = P("gx", "gy", "gz")
    pair = P(None, "gx", "gy", "gz")
    return jax.shard_map(
        body,
        mesh=mesh,
        in_specs=(cells, pair, pair, cells, cells, cells, cells, cells),
        out_specs=P(None, AXES, None),
        check_vma=False,
    )
```

```python
import jax
import jax.numpy as jnp
from jax import lax
from jax.experimental import pallas as pl
from jax.experimental.pallas import tpu as pltpu
from jax.sharding import PartitionSpec as P

AXES = ("gx", "gy", "gz")
F32 = jnp.float32
T = 32
L = 128
H = 10
OJ = 12
EI = T + 2 * H
EJ = 56
SWEEPS = 9
SLOTS = 640
ZG = 10
NQ = 5
SOLVE_MIB = 20
PAD = 8
ZS = 12


def strip_offsets():
    offsets, at = {}, 0
    for side in (0, 1):
        for dist in range(1, H):
            offsets[side, dist] = at
            at += H - dist
    return offsets


STRIPS = strip_offsets()


def plane_of(side, dist):
    return H - dist if side == 0 else dist - 1


def prep_kernel(
    p_far, sat_far, perm_far, sto_far, mask_far, own, xm, xp, ym, yp, p, sat, perm, sto, mask, sems
):
    pieces = 4
    many = T // pieces

    def copies(n):
        at = pl.ds(n * many, many)
        pairs = [(p_far.at[at], p.at[at]), (perm_far.at[at], perm.at[at])]
        pairs += [(sto_far.at[at], sto.at[at]), (mask_far.at[at], mask.at[at])]
        pairs += [(sat_far.at[:, at], sat.at[:, at])]
        return [
            pltpu.make_async_copy(far, near, sems.at[n, k]) for k, (far, near) in enumerate(pairs)
        ]

    def rows(q, carry):
        for u in range(4):
            i = q * 4 + u
            act = mask[i].astype(F32)
            s_w, s_g = sat[0, i], sat[1, i]
            s_o = 1.0 - s_w - s_g
            m_w, m_o, m_g = s_w * s_w * 2.0, s_o * s_o * 0.5, s_g * s_g * 4.0
            lam = m_w + m_o + m_g
            cond = perm[i] * act
            diag = act * (sto[i] * (0.5 * s_w + s_o + 2.0 * s_g)) + 3.0 * (1.0 - act)
            a_w, a_g = m_w / lam, m_g / lam
            for f, v in enumerate((cond, lam, diag, a_w, a_g)):
                own[f, i] = v
            for f, v in enumerate((p[i], cond, lam, diag)):
                ym[f * 8 + q, 10 * u : 10 * u + 10] = v[:H]
                yp[f * 8 + q, 10 * u : 10 * u + 10] = v[T - H :]
            for f, v in enumerate((a_w, a_g)):
                ym[32 + f, pl.ds(i, 1)] = v[:1]
                yp[32 + f, pl.ds(i, 1)] = v[T - 1 :]
        return carry

    for n in range(pieces):
        for copy in copies(n):
            copy.start()
    for n in range(pieces):
        for copy in copies(n):
            copy.wait()
        lax.fori_loop(n * many // 4, (n + 1) * many // 4, rows, 0)
    for f in range(4):
        for t in range(H):
            xm[f * H + t] = p[t] if f == 0 else own[f - 1, t]
            xp[f * H + t] = p[T - H + t] if f == 0 else own[f - 1, T - H + t]
    for f in range(2):
        xm[4 * H + f] = own[3 + f, 0]
        xp[4 * H + f] = own[3 + f, T - 1]


def strip_kernel(dst, x_lo, x_hi, places, cm, cp):
    del dst, places
    for f in range(4):
        for side, src in ((0, x_lo), (1, x_hi)):
            for dist in range(1, H):
                n, at = H - dist, STRIPS[side, dist]
                t = f * H + plane_of(side, dist)
                cm[f, at : at + n] = src[t, :n]
                cp[f, at : at + n] = src[t, T - n :]


def lanes_of(rows):
    return lax.broadcasted_iota(jnp.int32, (rows, L), 1)


def up(v):
    return pltpu.roll(v, v.shape[0] - 1, 0)


def down(v):
    return pltpu.roll(v, 1, 0)


def turn(v, by):
    return pltpu.roll(v, by % L if isinstance(by, int) else lax.rem(by + 2 * L, L), 1)


def build_kernel(edge, p, own, x_lo, x_hi, y_lo, y_hi, c_lo, c_hi, ext, aext, zm, zp):
    def cells(q, carry):
        for u in range(4):
            i = q * 4 + u
            for f in range(4):
                lo = y_lo[f * 8 + q, 10 * u : 10 * u + 10]
                hi = y_hi[f * 8 + q, 10 * u : 10 * u + 10]
                if f == 1:
                    lo, hi = lo * edge[2], hi * edge[3]
                ext[f, H + i, OJ - H : OJ] = lo
                ext[f, H + i, OJ : OJ + T] = p[i] if f == 0 else own[f - 1, i]
                ext[f, H + i, OJ + T : OJ + T + H] = hi
            for f in range(2):
                aext[f, 1 + i, OJ - 1 : OJ] = y_lo[32 + f, pl.ds(i, 1)]
                aext[f, 1 + i, OJ : OJ + T] = own[3 + f, i]
                aext[f, 1 + i, OJ + T : OJ + T + 1] = y_hi[32 + f, pl.ds(i, 1)]
        return carry

    lax.fori_loop(0, 8, cells, 0)
    for f in range(4):
        for side, src in ((0, x_lo), (1, x_hi)):
            for dist in range(1, H + 1):
                t = plane_of(side, dist)
                i = t if side == 0 else H + T + t
                v = src[f * H + t]
                if f == 1:
                    v = v * edge[side]
                ext[f, i, OJ : OJ + T] = v
                n = H - dist
                if n:
                    at = STRIPS[side, dist]
                    lo, hi = c_lo[f, at : at + n], c_hi[f, at : at + n]
                    if f == 1:
                        lo, hi = lo * (edge[side] * edge[2]), hi * (edge[side] * edge[3])
                    ext[f, i, OJ - n : OJ] = lo
                    ext[f, i, OJ + T : OJ + T + n] = hi
    for f in range(2):
        aext[f, 0, OJ : OJ + T] = x_lo[4 * H + f]
        aext[f, T + 1, OJ : OJ + T] = x_hi[4 * H + f]
    lane = lanes_of(EJ)

    def pack(s, carry):
        f, q = s // NQ, s % NQ
        low = jnp.zeros((EJ, L), F32)
        high = low
        for g in range(ZG):
            i = 1 + q + NQ * g
            r = ext[f, i, :EJ]
            if g:
                r = turn(r, ZS * g)
                ext[f, i, :EJ] = r
            low = jnp.where((lane >= ZS * g) & (lane < ZS * g + H), r, low)
            first = (ZS * g - H) % L
            high = jnp.where((lane >= first) & (lane < first + H), r, high)
        zm[s] = low
        zp[s] = high
        return carry

    lax.fori_loop(0, 4 * NQ, pack, 0)
    for f in range(3):
        ext[f, EI - 1, :EJ] = turn(ext[f, EI - 1, :EJ], ZS * ZG)

    def pack_share(f, carry):
        low = jnp.zeros((EJ, L), F32)
        high = low
        for i in range(T + 2):
            v = aext[f, i]
            if 1 <= i <= T:
                spot = 2 * (i - 1)
                r = turn(v, spot) if spot else v
                low = jnp.where(lane == spot, r, low)
                high = jnp.where(lane == (spot + L - 1) % L, r, high)
            aext[f, i] = turn(v, ZS * ((i + H - 2) // NQ))
        zm[4 * NQ + f] = low
        zp[4 * NQ + f] = high
        return carry

    lax.fori_loop(0, 2, pack_share, 0)


def face(p, c, m, pn, cn, mn):
    trans = 2.0 * c * cn / jnp.maximum(c + cn, 0.5)
    there = trans * jnp.where(p >= pn, m, mn)
    back = trans * jnp.where(pn >= p, mn, m)
    step = pn - p
    return there, back, there * step, back * step


def combine(diag, x, x_carry, y, z, z_back, z_bflow):
    y_back, y_bflow = down(y[1]), down(y[3])
    whole = diag + (x[0] + x_carry[0]) + (y[0] + y_back) + (z[0] + z_back)
    flow = (x[2] - x_carry[1]) + (y[2] - y_bflow) + (z[2] - z_bflow)
    inv = 1.0 / whole
    weights = [w * inv for w in (x[0], x_carry[0], y[0], y_back, z[0], z_back)]
    return whole, flow * inv, weights


def assemble_kernel(ext, mat, base, total):
    rows_all, rows_up = slice(0, EJ), slice(1, EJ + 1)

    def group(g, carry):
        for q in range(NQ):
            i = 1 + NQ * g + q
            here = [ext[f, i, rows_all] for f in range(3)]
            ahead = [ext[f, i + 1, rows_all] for f in range(3)]
            if q == NQ - 1:
                ahead = [turn(v, -ZS) for v in ahead]
            x = face(*here, *ahead)
            y = face(*here, *(ext[f, i, rows_up] for f in range(3)))
            z = face(*here, *(turn(v, -1) for v in here))
            whole, start, weights = combine(
                ext[3, i, rows_all], x, carry, y, z, turn(z[1], 1), turn(z[3], 1)
            )
            for k, w in enumerate(weights):
                mat[k, i] = w
            total[i] = whole
            base[i, PAD : PAD + EJ] = start
            carry = x[1], x[3]
        return tuple(turn(v, ZS) for v in carry)

    x = face(*(ext[f, 0, rows_all] for f in range(3)), *(ext[f, 1, rows_all] for f in range(3)))
    lax.fori_loop(0, ZG, group, (x[1], x[3]))


def solve_kernel(
    edge, dst, ext, aext, z_lo, z_hi, z_first, z_last, sat, old, sto, mask, places,
    mat_in, base_in, total_in, send, mat, base, total,
    side, rim, zmat, ztotal, one, two, zbase, zone, ztwo, border, share, stage,
):
    del mat_in, base_in, total_in
    lane = lanes_of(EJ)
    part = lax.rem(lane, ZS)
    first_lane = (part < 2) & (lane < ZS * ZG)
    last_lane = part >= ZS - 2
    for late in (L - 2, L - 1):
        last_lane = last_lane | (lane == late)
    start_lane = part == 0
    body_rows = slice(PAD, PAD + EJ)

    def wrap(ref, t):
        ref[t, 0] = turn(ref[t, NQ], ZS)
        ref[t, NQ + 1] = turn(ref[t, 1], -ZS)

    def join(q, carry):
        for f in range(4):
            right, left = z_hi[f * NQ + q], z_lo[f * NQ + q]
            if f == 1:
                right, left = right * edge[5], left * edge[4]
            if f == 0:
                rim[q] = jnp.where(start_lane, right, left)
            side[f, 0, 1 + q] = jnp.where(last_lane, z_last[f * NQ + q], right)
            side[f, 1, 1 + q] = jnp.where(first_lane, z_first[f * NQ + q], left)
        return carry

    lax.fori_loop(0, NQ, join, 0)
    for f in range(3):
        for t in (0, 1):
            wrap(side.at[f], t)

    for t in (0, 1):

        def packed(q, carry, t=t):
            here = [side[f, t, q] for f in range(3)]
            x = face(*here, *(side[f, t, q + 1] for f in range(3)))
            y = face(*here, *(up(v) for v in here))
            z = face(*here, *(turn(v, -1) for v in here))
            whole, start, weights = combine(
                side[3, t, q], x, carry, y, z, turn(z[1], 1), turn(z[3], 1)
            )
            for k, w in enumerate(weights):
                zmat[k, t, q - 1] = w
            ztotal[t, q - 1] = whole
            zbase[t, q, body_rows] = start
            return x[1], x[3]

        x = face(*(side[f, t, 0] for f in range(3)), *(side[f, t, 1] for f in range(3)))
        lax.fori_loop(1, NQ + 1, packed, (x[1], x[3]))

    def spots(g, lanes):
        return lanes == ZS * g, lanes == lax.rem(ZS * g + L - 1, L)

    def ghosts(ref, q, value, rows_at, marks):
        pltpu.store(ref.at[0, 1 + q, rows_at], value, mask=marks[1])
        pltpu.store(ref.at[1, 1 + q, rows_at], value, mask=marks[0])

    def mend(q, carry):
        ends = [jnp.where(start_lane, zmat[k, 1, q], zmat[k, 0, q]) for k in range(6)]
        ends.append(jnp.where(start_lane, ztotal[1, q], ztotal[0, q]))
        start = jnp.where(start_lane, zbase[1, 1 + q, body_rows], zbase[0, 1 + q, body_rows])
        for g in range(ZG):
            i = 1 + NQ * g + q
            here = (lane == ZS * g) | (lane == (ZS * g + L - 1) % L)
            for k in range(6):
                pltpu.store(mat.at[k, i], ends[k], mask=here)
            if 1 <= g < ZG - 1:
                pltpu.store(total.at[i], ends[6], mask=here)
            pltpu.store(base.at[i, body_rows], start, mask=here)
        return carry

    lax.fori_loop(0, NQ, mend, 0)

    def prepare(zsrc):
        for t in (0, 1):
            wrap(zsrc, t)

        def plane(q, carry):
            border[q] = jnp.where(
                start_lane, zsrc[0, 1 + q, body_rows], zsrc[1, 1 + q, body_rows]
            )
            return carry

        lax.fori_loop(0, NQ, plane, 0, unroll=NQ)

    def sweep(src, zsrc, target, ztarget, depth):
        low, high = (4, 52) if depth > 4 else (8, 48)
        at = slice(low, high)
        y_at = slice(PAD + low, PAD + high)
        y_up, y_down = (slice(y_at.start + k, y_at.stop + k) for k in (1, -1))
        lanes = lanes_of(high - low)
        prepare(zsrc)

        def halo(q, carry):
            for t in (0, 1):
                y = zsrc[t, q, y_at]
                acc = zbase[t, q, y_at] + zmat[0, t, q - 1, at] * zsrc[t, q + 1, y_at]
                acc = acc + zmat[1, t, q - 1, at] * zsrc[t, q - 1, y_at]
                acc = acc + zmat[2, t, q - 1, at] * zsrc[t, q, y_up]
                acc = acc + zmat[3, t, q - 1, at] * zsrc[t, q, y_down]
                acc = acc + zmat[4, t, q - 1, at] * turn(y, -1)
                ztarget[t, q, y_at] = acc + zmat[5, t, q - 1, at] * turn(y, 1)
            return carry

        lax.fori_loop(1, NQ + 1, halo, 0, unroll=NQ)

        def planes(g, carry):
            marks = spots(g, lanes)
            for q in range(NQ):
                i = 1 + NQ * g + q
                y, near = src[i, y_at], border[q, at]
                ahead, behind = src[i + 1, y_at], src[i - 1, y_at]
                if q == 0:
                    behind = turn(behind, ZS)
                if q == NQ - 1:
                    ahead = turn(ahead, -ZS)
                acc = base[i, y_at] + mat[0, i, at] * ahead
                acc = acc + mat[1, i, at] * behind
                acc = acc + mat[2, i, at] * src[i, y_up]
                acc = acc + mat[3, i, at] * src[i, y_down]
                acc = acc + mat[4, i, at] * turn(jnp.where(marks[0], near, y), -1)
                acc = acc + mat[5, i, at] * turn(jnp.where(marks[1], near, y), 1)
                target[i, y_at] = acc
                ghosts(ztarget, q, acc, y_at, marks)
            return carry

        groups = (0, ZG) if depth > 4 else (1, ZG - 1)
        lax.fori_loop(*groups, planes, 0, unroll=(groups[1] - groups[0]) // 2)

    src, zsrc = base, zbase
    for k in range(1, SWEEPS):
        target, ztarget = (one, zone) if k % 2 else (two, ztwo)
        sweep(src, zsrc, target, ztarget, SWEEPS - k)
        src, zsrc = target, ztarget
    prepare(zsrc)

    half = T // 2
    lanes = lanes_of(half)
    tile = slice(OJ, OJ + T)
    even = lax.rem(lanes_of(T), 2) == 0
    for f in range(2):
        share[f] = jnp.where(even, z_hi[4 * NQ + f, tile], z_lo[4 * NQ + f, tile])

    def moved(ref, lead, i, first, edge_plane, q, marks):
        at = slice(first, first + half)
        here = ref[lead + (i, at)]
        out = {
            4: turn(jnp.where(marks[0], edge_plane, here), -1),
            5: turn(jnp.where(marks[1], edge_plane, here), 1),
        }
        if q == 0:
            out[1] = turn(ref[lead + (i - 1, at)], ZS)
        if q == NQ - 1:
            out[0] = turn(ref[lead + (i + 1, at)], -ZS)
        return out

    def near_of(ref, lead, i, first, ready):
        spots_of = ((1, 0), (-1, 0), (0, 1), (0, -1))
        return [
            ready[k] if k in ready else ref[lead + (i + d, slice(first + r, first + r + half))]
            for k, (d, r) in enumerate(spots_of)
        ] + [ready[4], ready[5]]

    def prefetch(g, q, marks, part):
        e = 1 + NQ * g + q
        i = e - H
        first = OJ + half * part
        at, own = slice(first, first + half), slice(half * part, half * part + half)
        edges = [turn(share[f, own], ZS * g - 2 * i) for f in range(2)]
        return [
            moved(ext, (0,), e, first, rim[q, at], q, marks),
            moved(src, (), e, PAD + first, border[q, at], q, marks),
        ] + [moved(aext, (f,), i + 1, first, edges[f], q, marks) for f in range(2)]

    def finish(g, q, part, ready):
        e = 1 + NQ * g + q
        i = e - H
        first = OJ + half * part
        at, y_at = slice(first, first + half), slice(PAD + first, PAD + first + half)
        own = slice(half * part, half * part + half)
        pa = ext[0, e, at]
        p_near = near_of(ext, (0,), e, first, ready[0])
        s_near = near_of(src, (), e, PAD + first, ready[1])
        shares = [
            (aext[f, i + 1, at], near_of(aext, (f,), i + 1, first, ready[2 + f]))
            for f in range(2)
        ]
        x_p = base[e, y_at]
        column = [None, None]
        drive = [None, None]
        for k in range(6):
            weight = mat[k, e, at]
            x_p = x_p + weight * s_near[k]
            upstream = pa >= p_near[k]
            step = s_near[k] - (pa - p_near[k])
            for f, (a, a_near) in enumerate(shares):
                w = weight * jnp.where(upstream, a, a_near[k])
                column[f] = w if k == 0 else column[f] + w
                drive[f] = w * step if k == 0 else drive[f] + w * step
        scale = total[e, at]
        shift = -ZS * g
        coupled = [turn((drive[f] - column[f] * x_p) * scale, shift) for f in range(2)]
        return turn(x_p, shift), coupled

    def settle(g, q, part, result):
        i = 1 + NQ * g + q - H
        own = slice(half * part, half * part + half)
        x_p, coupled = result
        act = mask[i, own].astype(F32)
        held = act * sto[i, own]
        idle = 1.0 - act
        inverse = 1.0 / (held + idle)
        stage[0, i, own] = x_p
        for f, compress in ((0, 0.5), (1, 2.0)):
            s_now = sat[f, i, own]
            local = (held * (compress * s_now) + idle) * x_p
            change = held * (s_now - old[f, i, own])
            stage[1 + f, i, own] = (coupled[f] - change - local) * inverse

    def chain(items):
        ready, result = prefetch(*items[0]), None
        for n, (g, q, marks, part) in enumerate(items):
            later = prefetch(*items[n + 1]) if n + 1 < len(items) else None
            now = finish(g, q, part, ready)
            if n:
                settle(items[n - 1][0], items[n - 1][1], items[n - 1][3], result)
            ready, result = later, now
        settle(items[-1][0], items[-1][1], items[-1][3], result)

    def group(g, carry):
        marks = spots(g, lanes)
        chain([(g, q, marks, part) for q in range(NQ) for part in (0, 1)])
        return carry

    lax.fori_loop(2, 8, group, 0)
    chain([
        (jnp.int32(g), q, spots(g, lanes), part)
        for g, q in ((1, NQ - 1), (8, 0))
        for part in (0, 1)
    ])

    devices = places.shape[0]
    capacity = T * T // devices
    chunk = 3 * capacity + 1

    def place(i, carry):
        for j in range(T):
            d = dst[i * T + j]
            for f in range(3):
                send[pl.ds(d + f * capacity, 1)] = stage[f, i, j : j + 1]
        return carry

    lax.fori_loop(0, T, place, 0, unroll=4)

    def tail(d, carry):
        send[pl.ds(d * chunk + 3 * capacity, 1)] = places[pl.ds(d, 1)]
        return carry

    lax.fori_loop(0, devices, tail, 0, unroll=8)


def index_kernel(owner, slot, dst, places):
    devices = places.shape[0]
    capacity = T * T // devices
    chunk = 3 * capacity + 1
    bf16 = jnp.bfloat16
    who = lax.broadcasted_iota(jnp.int32, (devices, L), 0)
    spot = lax.broadcasted_iota(jnp.int32, (L, L), 0)
    earlier = (spot < lax.broadcasted_iota(jnp.int32, (L, L), 1)).astype(F32).astype(bf16)
    count = jnp.zeros((devices, 1), F32)
    coarse = jnp.zeros((devices, L), F32)
    fine = coarse
    for c in range(T * T // L):
        own = owner[c : c + 1]
        hit = (who == own).astype(F32)
        ahead = jnp.dot(hit.astype(bf16), earlier, preferred_element_type=F32) + count
        count = count + jnp.sum(hit, axis=1, keepdims=True)
        rank = jnp.sum(hit * ahead, axis=0, keepdims=True).astype(jnp.int32)
        dst[c : c + 1] = jnp.where(own >= 0, own * chunk + rank, -1)
        place = slot[c : c + 1]
        high = lax.div(place, 32)
        here = spot == rank
        for part, value in enumerate((high, place - 32 * high)):
            row = jnp.where(here, value.astype(F32), 0.0).astype(bf16)
            found = lax.dot_general(
                hit.astype(bf16), row, (((1,), (1,)), ((), ())), preferred_element_type=F32
            )
            if part == 0:
                coarse = coarse + found
            else:
                fine = fine + found
    free = jnp.where(count < capacity, lax.broadcasted_iota(jnp.int32, (devices, 1), 0).astype(F32), 0.0)
    spare = jnp.max(free, axis=0, keepdims=True).astype(jnp.int32) * chunk + capacity - 1
    dst[...] = jnp.where(dst[...] < 0, spare, dst[...])
    lane = lax.broadcasted_iota(jnp.int32, (devices, L), 1).astype(F32)
    places[...] = jnp.where(lane < count, 32.0 * coarse + fine, -1.0)


def unpack_kernel(got, update, held, number, table, where, sem):
    devices = where.shape[0]
    capacity = T * T // devices
    chunk = 3 * capacity + 1

    def collect(d, carry):
        number[pl.ds(d, 1)] = got[pl.ds(d * chunk + 3 * capacity, 1)]
        return carry

    lax.fori_loop(0, devices, collect, 0, unroll=8)
    slots = number[...].astype(jnp.int32)
    table[...] = jnp.where(slots < 0, SLOTS, slots)
    copy = pltpu.make_async_copy(table, where, sem)
    copy.start()
    copy.wait()

    def scatter(d, carry):
        for k in range(capacity):
            s = where[d, k]
            for f in range(3):
                held[f, pl.ds(s, 1)] = got[pl.ds(d * chunk + f * capacity + k, 1)]
        return carry

    lax.fori_loop(0, devices, scatter, 0, unroll=8)
    copy = pltpu.make_async_copy(held.at[:, :SLOTS], update, sem)
    copy.start()
    copy.wait()


def spec(space):
    return pl.BlockSpec(memory_space=space)


def shape(*dims):
    return jax.ShapeDtypeStruct(dims, F32)


def call(kernel, name, out_shape, smem, count, out_spaces=None, scratch=(), limit=16, alias=None, space=pltpu.VMEM):
    many = isinstance(out_shape, (tuple, list))
    spaces = out_spaces or ([pltpu.VMEM] * len(out_shape) if many else pltpu.VMEM)
    return pl.pallas_call(
        kernel,
        name=name,
        out_shape=out_shape,
        in_specs=[spec(pltpu.SMEM)] * smem + [spec(space)] * count,
        out_specs=[spec(s) for s in spaces] if many else spec(spaces),
        scratch_shapes=list(scratch),
        input_output_aliases=alias or {},
        compiler_params=pltpu.CompilerParams(vmem_limit_bytes=limit << 20),
    )


def ring(axis, step):
    size = lax.axis_size(axis)
    return [(i, (i + step) % size) for i in range(size)]


def swap(low, high, axis):
    return lax.ppermute(high, axis, ring(axis, 1)), lax.ppermute(low, axis, ring(axis, -1))


def body(
    pressure, saturation, old_saturation, permeability, storage, cell_mask, row_owner, row_slot
):
    devices = lax.axis_size(AXES)
    capacity = T * T // devices
    chunk = 3 * capacity + 1
    inside = []
    for axis in AXES:
        at = lax.axis_index(axis)
        inside += [at > 0, at < lax.axis_size(axis) - 1]
    edge = jnp.stack(inside).astype(F32)

    own, xm, xp, ym, yp = call(
        prep_kernel,
        "prep",
        (
            shape(5, T, T, L),
            shape(4 * H + 2, T, L),
            shape(4 * H + 2, T, L),
            shape(34, 40, L),
            shape(34, 40, L),
        ),
        0,
        5,
        None,
        [pltpu.VMEM((T, T, L), F32), pltpu.VMEM((2, T, T, L), F32)]
        + [pltpu.VMEM((T, T, L), F32)] * 2
        + [pltpu.VMEM((T, T, L), jnp.int32), pltpu.SemaphoreType.DMA((4, 5))],
        60,
        space=pltpu.HBM,
    )(pressure, saturation, permeability, storage, cell_mask)
    x_lo, x_hi = swap(xm, xp, "gx")
    y_lo, y_hi = swap(ym, yp, "gy")

    table = (T * T // L, L)
    dst, places = call(
        index_kernel, "index", (jax.ShapeDtypeStruct(table, jnp.int32), shape(devices, L)), 0, 2
    )(row_owner.reshape(table), row_slot.reshape(table))
    dst = dst.reshape(T * T)

    cm, cp = call(strip_kernel, "strip", (shape(4, 96, L), shape(4, 96, L)), 1, 3)(
        dst, x_lo, x_hi, places
    )
    c_lo, c_hi = swap(cm, cp, "gy")
    ext, aext, zm, zp = call(
        build_kernel,
        "build",
        (shape(4, EI, EJ + 8, L), shape(2, T + 2, EJ, L), shape(22, EJ, L), shape(22, EJ, L)),
        1,
        8,
        limit=24,
    )(edge, pressure, own, x_lo, x_hi, y_lo, y_hi, c_lo, c_hi)
    z_lo, z_hi = swap(zm, zp, "gz")
    grid, tall = (EI, EJ, L), (EI, EJ + 2 * PAD, L)
    rows_of = (shape(6, *grid), shape(*tall), shape(*grid))
    mat, base, total = call(assemble_kernel, "assemble", rows_of, 0, 1)(ext)
    send, *_ = call(
        solve_kernel,
        "solve",
        (shape(devices * chunk, L),) + rows_of,
        2,
        14,
        None,
        [
            pltpu.VMEM((4, 2, NQ + 2, EJ, L), F32),
            pltpu.VMEM((NQ, EJ, L), F32),
            pltpu.VMEM((6, 2, NQ, EJ, L), F32),
            pltpu.VMEM((2, NQ, EJ, L), F32),
        ]
        + [pltpu.VMEM(tall, F32)] * 2
        + [pltpu.VMEM((2, NQ + 2, EJ + 2 * PAD, L), F32)] * 3
        + [
            pltpu.VMEM((NQ, EJ, L), F32),
            pltpu.VMEM((2, T, L), F32),
            pltpu.VMEM((3, T, T, L), F32),
        ],
        SOLVE_MIB,
        {13: 1, 14: 2, 15: 3},
    )(
        edge, dst, ext, aext, z_lo, z_hi, zm, zp,
        saturation, old_saturation, storage, cell_mask, places, mat, base, total,
    )
    got = lax.all_to_all(
        send.reshape(devices, chunk, 1, L), AXES, split_axis=0, concat_axis=0, tiled=True
    )
    return call(
        unpack_kernel,
        "unpack",
        shape(3, SLOTS, L),
        0,
        1,
        pl.ANY,
        [
            pltpu.VMEM((3, SLOTS + 8, L), F32),
            pltpu.VMEM((devices, L), F32),
            pltpu.VMEM((devices, L), jnp.int32),
            pltpu.SMEM((devices, L), jnp.int32),
            pltpu.SemaphoreType.DMA(()),
        ],
    )(got.reshape(devices * chunk, L))


def solution(mesh):
    cells = P("gx", "gy", "gz")
    pair = P(None, "gx", "gy", "gz")
    return jax.shard_map(
        body,
        mesh=mesh,
        in_specs=(cells, pair, pair, cells, cells, cells, cells, cells),
        out_specs=P(None, AXES, None),
        check_vma=False,
    )
```

```python
import jax
import jax.numpy as jnp
from jax import lax
from jax.experimental import pallas as pl
from jax.experimental.pallas import tpu as pltpu
from jax.sharding import PartitionSpec as P

AXES = ("gx", "gy", "gz")
F32 = jnp.float32
T = 32
L = 128
H = 10
OJ = 12
EI = T + 2 * H
EJ = 56
SWEEPS = 9
SLOTS = 640
ZG = 10
NQ = 5
SOLVE_MIB = 20
LIMITS = {"index": 4, "strip": 6, "seed": 12, "flank": 16, "corner": 20, "assemble": 16, "unpack": 8}
PAD = 8
ZS = 12


def strip_offsets():
    offsets, at = {}, 0
    for side in (0, 1):
        for dist in range(1, H):
            offsets[side, dist] = at
            at += H - dist
    return offsets


STRIPS = strip_offsets()


def plane_of(side, dist):
    return H - dist if side == 0 else dist - 1


def prep_kernel(
    p_far, sat_far, perm_far, sto_far, mask_far, own, xm, xp, ym, yp, p, sat, perm, sto, mask, sems
):
    pieces = 4
    many = T // pieces

    def copies(n):
        at = pl.ds(n * many, many)
        pairs = [(p_far.at[at], p.at[at]), (perm_far.at[at], perm.at[at])]
        pairs += [(sto_far.at[at], sto.at[at]), (mask_far.at[at], mask.at[at])]
        pairs += [(sat_far.at[:, at], sat.at[:, at])]
        return [
            pltpu.make_async_copy(far, near, sems.at[n, k]) for k, (far, near) in enumerate(pairs)
        ]

    def rows(q, carry):
        for u in range(4):
            i = q * 4 + u
            act = mask[i].astype(F32)
            s_w, s_g = sat[0, i], sat[1, i]
            s_o = 1.0 - s_w - s_g
            m_w, m_o, m_g = s_w * s_w * 2.0, s_o * s_o * 0.5, s_g * s_g * 4.0
            lam = m_w + m_o + m_g
            cond = perm[i] * act
            diag = act * (sto[i] * (0.5 * s_w + s_o + 2.0 * s_g)) + 3.0 * (1.0 - act)
            a_w, a_g = m_w / lam, m_g / lam
            for f, v in enumerate((cond, lam, diag, a_w, a_g)):
                own[f, i] = v
            for f, v in enumerate((p[i], cond, lam, diag)):
                ym[f * 8 + q, 10 * u : 10 * u + 10] = v[:H]
                yp[f * 8 + q, 10 * u : 10 * u + 10] = v[T - H :]
            for f, v in enumerate((a_w, a_g)):
                ym[32 + f, pl.ds(i, 1)] = v[:1]
                yp[32 + f, pl.ds(i, 1)] = v[T - 1 :]
        return carry

    for n in range(pieces):
        for copy in copies(n):
            copy.start()
    for n in range(pieces):
        for copy in copies(n):
            copy.wait()
        lax.fori_loop(n * many // 4, (n + 1) * many // 4, rows, 0)
    for f in range(4):
        for t in range(H):
            xm[f * H + t] = p[t] if f == 0 else own[f - 1, t]
            xp[f * H + t] = p[T - H + t] if f == 0 else own[f - 1, T - H + t]
    for f in range(2):
        xm[4 * H + f] = own[3 + f, 0]
        xp[4 * H + f] = own[3 + f, T - 1]


def strip_kernel(dst, x_lo, x_hi, places, zm, cm, cp):
    del dst, places, zm
    for f in range(4):
        for side, src in ((0, x_lo), (1, x_hi)):
            for dist in range(1, H):
                n, at = H - dist, STRIPS[side, dist]
                t = f * H + plane_of(side, dist)
                cm[f, at : at + n] = src[t, :n]
                cp[f, at : at + n] = src[t, T - n :]


def lanes_of(rows):
    return lax.broadcasted_iota(jnp.int32, (rows, L), 1)


def up(v):
    return pltpu.roll(v, v.shape[0] - 1, 0)


def down(v):
    return pltpu.roll(v, 1, 0)


def turn(v, by):
    if isinstance(by, int):
        return pltpu.roll(v, by % L, 1) if by % L else v
    return pltpu.roll(v, lax.rem(by + 2 * L, L), 1)


MID = slice(OJ, OJ + T)


def packing(g, rows):
    lane = lanes_of(rows)
    first = lane - ZS * g
    last = lane - (ZS * g - H) % L if isinstance(g, int) else lane - lax.rem(ZS * g + L - H, L)
    return (first >= 0) & (first < H), (last >= 0) & (last < H)


def put(ext, zm, zp, f, i, rows, value, masks):
    if isinstance(i, int):
        q, g = (i - 1) % NQ, (i - 1) // NQ
    else:
        q, g = lax.rem(i - 1, NQ), lax.div(i - 1, NQ)
    r = turn(value, ZS * g)
    ext[f, i, rows] = r
    pltpu.store(zm.at[f * NQ + q, rows], r, mask=masks[0])
    pltpu.store(zp.at[f * NQ + q, rows], r, mask=masks[1])


def seed_kernel(p, own, turned, aext, zm, zp):
    lane = lanes_of(T)

    def plane(i, carry):
        e = i + H
        g = lax.div(e - 1, NQ)
        masks = packing(g, T)
        for f in range(4):
            r = turn(p[i] if f == 0 else own[f - 1, i], ZS * g)
            turned[f, i] = r
            s = f * NQ + lax.rem(e - 1, NQ)
            pltpu.store(zm.at[s, MID], r, mask=masks[0])
            pltpu.store(zp.at[s, MID], r, mask=masks[1])
        spot = 2 * i
        for f in range(2):
            v = own[3 + f, i]
            aext[f, i] = turn(v, ZS * g)
            r = turn(v, spot)
            pltpu.store(zm.at[4 * NQ + f, MID], r, mask=lane == spot)
            pltpu.store(zp.at[4 * NQ + f, MID], r, mask=lane == lax.rem(spot + L - 1, L))
        return carry

    lax.fori_loop(0, T, plane, 0, unroll=4)


def flank_kernel(
    edge, y_lo, y_hi, x_lo, x_hi, turned, aext_in, zm_in, zp_in, ext, aext, zm, zp
):
    zm[...] = zm_in[...]
    zp[...] = zp_in[...]

    def planes(block, carry):
        for u in range(4):
            i = block * 4 + u
            e = i + H
            masks = packing(lax.div(e - 1, NQ), H)
            shift = ZS * lax.div(e - 1, NQ)
            for src, rows, k in (
                (y_lo, slice(OJ - H, OJ), 2),
                (y_hi, slice(OJ + T, OJ + T + H), 3),
            ):
                for f in range(4):
                    v = src[f * 8 + block, 10 * u : 10 * u + 10]
                    put(ext, zm, zp, f, e, rows, v * edge[k] if f == 1 else v, masks)
            for f in range(4):
                ext[f, e, MID] = turned[f, i]
            for f in range(2):
                aext[f, 1 + i, MID] = aext_in[f, i]
                aext[f, 1 + i, OJ - 1 : OJ] = turn(y_lo[32 + f, pl.ds(i, 1)], shift)
                aext[f, 1 + i, OJ + T : OJ + T + 1] = turn(y_hi[32 + f, pl.ds(i, 1)], shift)
        return carry

    lax.fori_loop(0, 8, planes, 0)
    for side, src in ((0, x_lo), (1, x_hi)):
        for dist in range(1, H + 1):
            t = plane_of(side, dist)
            i = t if side == 0 else H + T + t
            for f in range(4 if dist < H else 3):
                v = src[f * H + t]
                if f == 1:
                    v = v * edge[side]
                if dist < H:
                    put(ext, zm, zp, f, i, MID, v, packing((i - 1) // NQ, T))
                else:
                    ext[f, i, MID] = turn(v, 0 if side == 0 else ZS * ZG)
        for f in range(2):
            i = 0 if side == 0 else T + 1
            aext[f, i, MID] = turn(src[4 * H + f], ZS * ((i + H - 2) // NQ))


def corner_kernel(
    edge, c_lo, c_hi, ext_in, zm_in, zp_in, ext, zm, zp
):
    zm[...] = zm_in[...]
    zp[...] = zp_in[...]

    def carry_over(i, carry):
        for f in range(4):
            ext[f, i, :EJ] = ext_in[f, i, :EJ]
        return carry

    lax.fori_loop(0, EI, carry_over, 0)
    for side in (0, 1):
        for dist in range(1, H):
            t = plane_of(side, dist)
            i = t if side == 0 else H + T + t
            n, at = H - dist, STRIPS[side, dist]
            masks = packing((i - 1) // NQ, n)
            for f in range(4):
                lo, hi = c_lo[f, at : at + n], c_hi[f, at : at + n]
                if f == 1:
                    lo, hi = lo * (edge[side] * edge[2]), hi * (edge[side] * edge[3])
                put(ext, zm, zp, f, i, slice(OJ - n, OJ), lo, masks)
                put(ext, zm, zp, f, i, slice(OJ + T, OJ + T + n), hi, masks)


def face(p, c, m, pn, cn, mn):
    trans = 2.0 * c * cn / jnp.maximum(c + cn, 0.5)
    there = trans * jnp.where(p >= pn, m, mn)
    back = trans * jnp.where(pn >= p, mn, m)
    step = pn - p
    return there, back, there * step, back * step


def combine(diag, x, x_carry, y, z, z_back, z_bflow):
    y_back, y_bflow = down(y[1]), down(y[3])
    whole = diag + (x[0] + x_carry[0]) + (y[0] + y_back) + (z[0] + z_back)
    flow = (x[2] - x_carry[1]) + (y[2] - y_bflow) + (z[2] - z_bflow)
    inv = 1.0 / whole
    weights = [w * inv for w in (x[0], x_carry[0], y[0], y_back, z[0], z_back)]
    return whole, flow * inv, weights


def assemble_kernel(ext, mat, base, total):
    rows_all, rows_up = slice(0, EJ), slice(1, EJ + 1)

    def group(g, carry):
        for q in range(NQ):
            i = 1 + NQ * g + q
            here = [ext[f, i, rows_all] for f in range(3)]
            ahead = [ext[f, i + 1, rows_all] for f in range(3)]
            if q == NQ - 1:
                ahead = [turn(v, -ZS) for v in ahead]
            x = face(*here, *ahead)
            y = face(*here, *(ext[f, i, rows_up] for f in range(3)))
            z = face(*here, *(turn(v, -1) for v in here))
            whole, start, weights = combine(
                ext[3, i, rows_all], x, carry, y, z, turn(z[1], 1), turn(z[3], 1)
            )
            for k, w in enumerate(weights):
                mat[k, i] = w
            total[i] = whole
            base[i, PAD : PAD + EJ] = start
            carry = x[1], x[3]
        return tuple(turn(v, ZS) for v in carry)

    x = face(*(ext[f, 0, rows_all] for f in range(3)), *(ext[f, 1, rows_all] for f in range(3)))
    lax.fori_loop(0, ZG, group, (x[1], x[3]))


def solve_kernel(
    edge, dst, ext, aext, z_lo, z_hi, z_first, z_last, sat, old, sto, mask, places,
    mat_in, base_in, total_in, send, mat, base, total,
    side, rim, zmat, ztotal, one, two, zbase, zone, ztwo, border, share, stage,
):
    del mat_in, base_in, total_in
    lane = lanes_of(EJ)
    part = lax.rem(lane, ZS)
    first_lane = (part < 2) & (lane < ZS * ZG)
    last_lane = part >= ZS - 2
    for late in (L - 2, L - 1):
        last_lane = last_lane | (lane == late)
    start_lane = part == 0
    body_rows = slice(PAD, PAD + EJ)

    def wrap(ref, t):
        ref[t, 0] = turn(ref[t, NQ], ZS)
        ref[t, NQ + 1] = turn(ref[t, 1], -ZS)

    def join(q, carry):
        for f in range(4):
            right, left = z_hi[f * NQ + q], z_lo[f * NQ + q]
            if f == 1:
                right, left = right * edge[5], left * edge[4]
            if f == 0:
                rim[q] = jnp.where(start_lane, right, left)
            side[f, 0, 1 + q] = jnp.where(last_lane, z_last[f * NQ + q], right)
            side[f, 1, 1 + q] = jnp.where(first_lane, z_first[f * NQ + q], left)
        return carry

    lax.fori_loop(0, NQ, join, 0)
    for f in range(3):
        for t in (0, 1):
            wrap(side.at[f], t)

    for t in (0, 1):

        def packed(q, carry, t=t):
            here = [side[f, t, q] for f in range(3)]
            x = face(*here, *(side[f, t, q + 1] for f in range(3)))
            y = face(*here, *(up(v) for v in here))
            z = face(*here, *(turn(v, -1) for v in here))
            whole, start, weights = combine(
                side[3, t, q], x, carry, y, z, turn(z[1], 1), turn(z[3], 1)
            )
            for k, w in enumerate(weights):
                zmat[k, t, q - 1] = w
            ztotal[t, q - 1] = whole
            zbase[t, q, body_rows] = start
            return x[1], x[3]

        x = face(*(side[f, t, 0] for f in range(3)), *(side[f, t, 1] for f in range(3)))
        lax.fori_loop(1, NQ + 1, packed, (x[1], x[3]))

    def spots(g, lanes):
        return lanes == ZS * g, lanes == lax.rem(ZS * g + L - 1, L)

    def ghosts(ref, q, value, rows_at, marks):
        pltpu.store(ref.at[0, 1 + q, rows_at], value, mask=marks[1])
        pltpu.store(ref.at[1, 1 + q, rows_at], value, mask=marks[0])

    def mend(q, carry):
        ends = [jnp.where(start_lane, zmat[k, 1, q], zmat[k, 0, q]) for k in range(6)]
        ends.append(jnp.where(start_lane, ztotal[1, q], ztotal[0, q]))
        start = jnp.where(start_lane, zbase[1, 1 + q, body_rows], zbase[0, 1 + q, body_rows])
        for g in range(ZG):
            i = 1 + NQ * g + q
            here = (lane == ZS * g) | (lane == (ZS * g + L - 1) % L)
            for k in range(6):
                pltpu.store(mat.at[k, i], ends[k], mask=here)
            if 1 <= g < ZG - 1:
                pltpu.store(total.at[i], ends[6], mask=here)
            pltpu.store(base.at[i, body_rows], start, mask=here)
        return carry

    lax.fori_loop(0, NQ, mend, 0)

    def prepare(zsrc):
        for t in (0, 1):
            wrap(zsrc, t)

        def plane(q, carry):
            border[q] = jnp.where(
                start_lane, zsrc[0, 1 + q, body_rows], zsrc[1, 1 + q, body_rows]
            )
            return carry

        lax.fori_loop(0, NQ, plane, 0, unroll=NQ)

    def sweep(src, zsrc, target, ztarget, depth):
        low, high = (4, 52) if depth > 4 else (8, 48)
        at = slice(low, high)
        y_at = slice(PAD + low, PAD + high)
        y_up, y_down = (slice(y_at.start + k, y_at.stop + k) for k in (1, -1))
        lanes = lanes_of(high - low)
        prepare(zsrc)

        def halo(q, carry):
            for t in (0, 1):
                y = zsrc[t, q, y_at]
                acc = zbase[t, q, y_at] + zmat[0, t, q - 1, at] * zsrc[t, q + 1, y_at]
                acc = acc + zmat[1, t, q - 1, at] * zsrc[t, q - 1, y_at]
                acc = acc + zmat[2, t, q - 1, at] * zsrc[t, q, y_up]
                acc = acc + zmat[3, t, q - 1, at] * zsrc[t, q, y_down]
                acc = acc + zmat[4, t, q - 1, at] * turn(y, -1)
                ztarget[t, q, y_at] = acc + zmat[5, t, q - 1, at] * turn(y, 1)
            return carry

        lax.fori_loop(1, NQ + 1, halo, 0, unroll=NQ)

        def planes(g, carry):
            marks = spots(g, lanes)
            for q in range(NQ):
                i = 1 + NQ * g + q
                y, near = src[i, y_at], border[q, at]
                ahead, behind = src[i + 1, y_at], src[i - 1, y_at]
                if q == 0:
                    behind = turn(behind, ZS)
                if q == NQ - 1:
                    ahead = turn(ahead, -ZS)
                acc = base[i, y_at] + mat[0, i, at] * ahead
                acc = acc + mat[1, i, at] * behind
                acc = acc + mat[2, i, at] * src[i, y_up]
                acc = acc + mat[3, i, at] * src[i, y_down]
                acc = acc + mat[4, i, at] * turn(jnp.where(marks[0], near, y), -1)
                acc = acc + mat[5, i, at] * turn(jnp.where(marks[1], near, y), 1)
                target[i, y_at] = acc
                ghosts(ztarget, q, acc, y_at, marks)
            return carry

        groups = (0, ZG) if depth > 4 else (1, ZG - 1)
        lax.fori_loop(*groups, planes, 0, unroll=(groups[1] - groups[0]) // 2)

    src, zsrc = base, zbase
    for k in range(1, SWEEPS):
        target, ztarget = (one, zone) if k % 2 else (two, ztwo)
        sweep(src, zsrc, target, ztarget, SWEEPS - k)
        src, zsrc = target, ztarget
    prepare(zsrc)

    half = T // 2
    lanes = lanes_of(half)
    tile = slice(OJ, OJ + T)
    even = lax.rem(lanes_of(T), 2) == 0
    for f in range(2):
        share[f] = jnp.where(even, z_hi[4 * NQ + f, tile], z_lo[4 * NQ + f, tile])

    def moved(ref, lead, i, first, edge_plane, q, marks):
        at = slice(first, first + half)
        here = ref[lead + (i, at)]
        out = {
            4: turn(jnp.where(marks[0], edge_plane, here), -1),
            5: turn(jnp.where(marks[1], edge_plane, here), 1),
        }
        if q == 0:
            out[1] = turn(ref[lead + (i - 1, at)], ZS)
        if q == NQ - 1:
            out[0] = turn(ref[lead + (i + 1, at)], -ZS)
        return out

    def near_of(ref, lead, i, first, ready):
        spots_of = ((1, 0), (-1, 0), (0, 1), (0, -1))
        return [
            ready[k] if k in ready else ref[lead + (i + d, slice(first + r, first + r + half))]
            for k, (d, r) in enumerate(spots_of)
        ] + [ready[4], ready[5]]

    def prefetch(g, q, marks, part):
        e = 1 + NQ * g + q
        i = e - H
        first = OJ + half * part
        at, own = slice(first, first + half), slice(half * part, half * part + half)
        edges = [turn(share[f, own], ZS * g - 2 * i) for f in range(2)]
        return [
            moved(ext, (0,), e, first, rim[q, at], q, marks),
            moved(src, (), e, PAD + first, border[q, at], q, marks),
        ] + [moved(aext, (f,), i + 1, first, edges[f], q, marks) for f in range(2)]

    def finish(g, q, part, ready):
        e = 1 + NQ * g + q
        i = e - H
        first = OJ + half * part
        at, y_at = slice(first, first + half), slice(PAD + first, PAD + first + half)
        own = slice(half * part, half * part + half)
        pa = ext[0, e, at]
        p_near = near_of(ext, (0,), e, first, ready[0])
        s_near = near_of(src, (), e, PAD + first, ready[1])
        shares = [
            (aext[f, i + 1, at], near_of(aext, (f,), i + 1, first, ready[2 + f]))
            for f in range(2)
        ]
        x_p = base[e, y_at]
        column = [None, None]
        drive = [None, None]
        for k in range(6):
            weight = mat[k, e, at]
            x_p = x_p + weight * s_near[k]
            upstream = pa >= p_near[k]
            step = s_near[k] - (pa - p_near[k])
            for f, (a, a_near) in enumerate(shares):
                w = weight * jnp.where(upstream, a, a_near[k])
                column[f] = w if k == 0 else column[f] + w
                drive[f] = w * step if k == 0 else drive[f] + w * step
        scale = total[e, at]
        shift = -ZS * g
        coupled = [turn((drive[f] - column[f] * x_p) * scale, shift) for f in range(2)]
        return turn(x_p, shift), coupled

    def settle(g, q, part, result):
        i = 1 + NQ * g + q - H
        own = slice(half * part, half * part + half)
        x_p, coupled = result
        act = mask[i, own].astype(F32)
        held = act * sto[i, own]
        idle = 1.0 - act
        inverse = 1.0 / (held + idle)
        stage[0, i, own] = x_p
        for f, compress in ((0, 0.5), (1, 2.0)):
            s_now = sat[f, i, own]
            local = (held * (compress * s_now) + idle) * x_p
            change = held * (s_now - old[f, i, own])
            stage[1 + f, i, own] = (coupled[f] - change - local) * inverse

    def chain(items):
        ready, result = prefetch(*items[0]), None
        for n, (g, q, marks, part) in enumerate(items):
            later = prefetch(*items[n + 1]) if n + 1 < len(items) else None
            now = finish(g, q, part, ready)
            if n:
                settle(items[n - 1][0], items[n - 1][1], items[n - 1][3], result)
            ready, result = later, now
        settle(items[-1][0], items[-1][1], items[-1][3], result)

    def group(g, carry):
        marks = spots(g, lanes)
        chain([(g, q, marks, part) for q in range(NQ) for part in (0, 1)])
        return carry

    lax.fori_loop(2, 8, group, 0)
    chain([
        (jnp.int32(g), q, spots(g, lanes), part)
        for g, q in ((1, NQ - 1), (8, 0))
        for part in (0, 1)
    ])

    devices = places.shape[0]
    capacity = T * T // devices
    chunk = 3 * capacity + 1

    def place(i, carry):
        for j in range(T):
            d = dst[i * T + j]
            for f in range(3):
                send[pl.ds(d + f * capacity, 1)] = stage[f, i, j : j + 1]
        return carry

    lax.fori_loop(0, T, place, 0, unroll=4)

    def tail(d, carry):
        send[pl.ds(d * chunk + 3 * capacity, 1)] = places[pl.ds(d, 1)]
        return carry

    lax.fori_loop(0, devices, tail, 0, unroll=8)


def index_kernel(owner, slot, dst, places):
    devices = places.shape[0]
    capacity = T * T // devices
    chunk = 3 * capacity + 1
    bf16 = jnp.bfloat16
    who = lax.broadcasted_iota(jnp.int32, (devices, L), 0)
    spot = lax.broadcasted_iota(jnp.int32, (L, L), 0)
    earlier = (spot < lax.broadcasted_iota(jnp.int32, (L, L), 1)).astype(F32).astype(bf16)
    count = jnp.zeros((devices, 1), F32)
    coarse = jnp.zeros((devices, L), F32)
    fine = coarse
    for c in range(T * T // L):
        own = owner[c : c + 1]
        hit = (who == own).astype(F32)
        ahead = jnp.dot(hit.astype(bf16), earlier, preferred_element_type=F32) + count
        count = count + jnp.sum(hit, axis=1, keepdims=True)
        rank = jnp.sum(hit * ahead, axis=0, keepdims=True).astype(jnp.int32)
        dst[c : c + 1] = jnp.where(own >= 0, own * chunk + rank, -1)
        place = slot[c : c + 1]
        high = lax.div(place, 32)
        here = spot == rank
        for part, value in enumerate((high, place - 32 * high)):
            row = jnp.where(here, value.astype(F32), 0.0).astype(bf16)
            found = lax.dot_general(
                hit.astype(bf16), row, (((1,), (1,)), ((), ())), preferred_element_type=F32
            )
            if part == 0:
                coarse = coarse + found
            else:
                fine = fine + found
    free = jnp.where(count < capacity, lax.broadcasted_iota(jnp.int32, (devices, 1), 0).astype(F32), 0.0)
    spare = jnp.max(free, axis=0, keepdims=True).astype(jnp.int32) * chunk + capacity - 1
    dst[...] = jnp.where(dst[...] < 0, spare, dst[...])
    lane = lax.broadcasted_iota(jnp.int32, (devices, L), 1).astype(F32)
    places[...] = jnp.where(lane < count, 32.0 * coarse + fine, -1.0)


def unpack_kernel(got, update, held, number, table, where, sem):
    devices = where.shape[0]
    capacity = T * T // devices
    chunk = 3 * capacity + 1

    def collect(d, carry):
        number[pl.ds(d, 1)] = got[pl.ds(d * chunk + 3 * capacity, 1)]
        return carry

    lax.fori_loop(0, devices, collect, 0, unroll=8)
    slots = number[...].astype(jnp.int32)
    table[...] = jnp.where(slots < 0, SLOTS, slots)
    copy = pltpu.make_async_copy(table, where, sem)
    copy.start()
    copy.wait()

    def scatter(d, carry):
        for k in range(capacity):
            s = where[d, k]
            for f in range(3):
                held[f, pl.ds(s, 1)] = got[pl.ds(d * chunk + f * capacity + k, 1)]
        return carry

    lax.fori_loop(0, devices, scatter, 0, unroll=8)
    copy = pltpu.make_async_copy(held.at[:, :SLOTS], update, sem)
    copy.start()
    copy.wait()


def spec(space):
    return pl.BlockSpec(memory_space=space)


def shape(*dims):
    return jax.ShapeDtypeStruct(dims, F32)


def call(kernel, name, out_shape, smem, count, out_spaces=None, scratch=(), limit=16, alias=None, space=pltpu.VMEM):
    many = isinstance(out_shape, (tuple, list))
    spaces = out_spaces or ([pltpu.VMEM] * len(out_shape) if many else pltpu.VMEM)
    return pl.pallas_call(
        kernel,
        name=name,
        out_shape=out_shape,
        in_specs=[spec(pltpu.SMEM)] * smem + [spec(space)] * count,
        out_specs=[spec(s) for s in spaces] if many else spec(spaces),
        scratch_shapes=list(scratch),
        input_output_aliases=alias or {},
        compiler_params=pltpu.CompilerParams(vmem_limit_bytes=LIMITS.get(name, limit) << 20),
    )


def ring(axis, step):
    size = lax.axis_size(axis)
    return [(i, (i + step) % size) for i in range(size)]


def swap(low, high, axis):
    return lax.ppermute(high, axis, ring(axis, 1)), lax.ppermute(low, axis, ring(axis, -1))


def body(
    pressure, saturation, old_saturation, permeability, storage, cell_mask, row_owner, row_slot
):
    devices = lax.axis_size(AXES)
    capacity = T * T // devices
    chunk = 3 * capacity + 1
    inside = []
    for axis in AXES:
        at = lax.axis_index(axis)
        inside += [at > 0, at < lax.axis_size(axis) - 1]
    edge = jnp.stack(inside).astype(F32)

    own, xm, xp, ym, yp = call(
        prep_kernel,
        "prep",
        (
            shape(5, T, T, L),
            shape(4 * H + 2, T, L),
            shape(4 * H + 2, T, L),
            shape(34, 40, L),
            shape(34, 40, L),
        ),
        0,
        5,
        None,
        [pltpu.VMEM((T, T, L), F32), pltpu.VMEM((2, T, T, L), F32)]
        + [pltpu.VMEM((T, T, L), F32)] * 2
        + [pltpu.VMEM((T, T, L), jnp.int32), pltpu.SemaphoreType.DMA((4, 5))],
        60,
        space=pltpu.HBM,
    )(pressure, saturation, permeability, storage, cell_mask)
    x_lo, x_hi = swap(xm, xp, "gx")
    y_lo, y_hi = swap(ym, yp, "gy")

    table = (T * T // L, L)
    dst, places = call(
        index_kernel, "index", (jax.ShapeDtypeStruct(table, jnp.int32), shape(devices, L)), 0, 2
    )(row_owner.reshape(table), row_slot.reshape(table))
    dst = dst.reshape(T * T)

    planes = (
        shape(4, EI, EJ + 8, L),
        shape(2, T + 2, EJ, L),
        shape(22, EJ, L),
        shape(22, EJ, L),
    )
    turned, tile_share, zm, zp = call(
        seed_kernel, "seed", (shape(4, T, T, L), shape(2, T, T, L)) + planes[2:], 0, 2
    )(pressure, own)
    cm, cp = call(strip_kernel, "strip", (shape(4, 96, L), shape(4, 96, L)), 1, 4)(
        dst, x_lo, x_hi, places, zm
    )
    c_lo, c_hi = swap(cm, cp, "gy")
    ext, aext, zm, zp = call(flank_kernel, "flank", planes, 1, 8)(
        edge, y_lo, y_hi, x_lo, x_hi, turned, tile_share, zm, zp
    )
    ext, zm, zp = call(corner_kernel, "corner", (planes[0], planes[2], planes[3]), 1, 5)(
        edge, c_lo, c_hi, ext, zm, zp
    )
    z_lo, z_hi = swap(zm, zp, "gz")
    grid, tall = (EI, EJ, L), (EI, EJ + 2 * PAD, L)
    rows_of = (shape(6, *grid), shape(*tall), shape(*grid))
    mat, base, total = call(assemble_kernel, "assemble", rows_of, 0, 1)(ext)
    send, *_ = call(
        solve_kernel,
        "solve",
        (shape(devices * chunk, L),) + rows_of,
        2,
        14,
        None,
        [
            pltpu.VMEM((4, 2, NQ + 2, EJ, L), F32),
            pltpu.VMEM((NQ, EJ, L), F32),
            pltpu.VMEM((6, 2, NQ, EJ, L), F32),
            pltpu.VMEM((2, NQ, EJ, L), F32),
        ]
        + [pltpu.VMEM(tall, F32)] * 2
        + [pltpu.VMEM((2, NQ + 2, EJ + 2 * PAD, L), F32)] * 3
        + [
            pltpu.VMEM((NQ, EJ, L), F32),
            pltpu.VMEM((2, T, L), F32),
            pltpu.VMEM((3, T, T, L), F32),
        ],
        SOLVE_MIB,
        {13: 1, 14: 2, 15: 3},
    )(
        edge, dst, ext, aext, z_lo, z_hi, zm, zp,
        saturation, old_saturation, storage, cell_mask, places, mat, base, total,
    )
    got = lax.all_to_all(
        send.reshape(devices, chunk, 1, L), AXES, split_axis=0, concat_axis=0, tiled=True
    )
    return call(
        unpack_kernel,
        "unpack",
        shape(3, SLOTS, L),
        0,
        1,
        pl.ANY,
        [
            pltpu.VMEM((3, SLOTS + 8, L), F32),
            pltpu.VMEM((devices, L), F32),
            pltpu.VMEM((devices, L), jnp.int32),
            pltpu.SMEM((devices, L), jnp.int32),
            pltpu.SemaphoreType.DMA(()),
        ],
    )(got.reshape(devices * chunk, L))


def solution(mesh):
    cells = P("gx", "gy", "gz")
    pair = P(None, "gx", "gy", "gz")
    return jax.shard_map(
        body,
        mesh=mesh,
        in_specs=(cells, pair, pair, cells, cells, cells, cells, cells),
        out_specs=P(None, AXES, None),
        check_vma=False,
    )
```
